32 devices in a mesh: rows: 16 (over z, x, core), cols: 2 (over y).
Axes of the slice: x: 2, y: 2, z: 4, core: 2. Of those that a mesh axis runs over, the one named last changes fastest.
Arguments:
- slab: float32 [131072, 512], P('rows', 'cols')
- sign_bits: int32 [131072], P('rows'), may hold values from 0 to 1
- block_mask: int32 [1024], P('rows'), may hold values 0 or 1
- sample_rows: int32 [2048], P('rows'), may hold values from 0 to 8191, as said below
Outputs:
- sketch_rows: float32 [2048, 512], P('rows', 'cols')
- r_factor: float32 [512, 512], P(None, 'cols')
The draws below stay inside these ranges and needn't reach their ends.
Inputs may be any that keep to these rules, and one draw needn't show every extreme that they name: `sample_rows`: each block of 128 entries names rows of the matching index of rows, as numbers below 8192; rows may repeat.
All inputs are finite; a program needn't handle non-finite values. No bound on the sum of `block_mask` on one device may be relied on, other than what follows from the above.
Results may differ from the reference program's by a relative error of at most 0.00016.
Values sent between devices are 32-bit elements; how exact they have to be, the bound alone decides.
No kernel may reach another device: no remote copies, remote signals or barrier semaphores. Data moves between devices by JAX's collectives and lax.ppermute only.
A program may use at most 64 MiB of HBM per device.

```python
import math
import jax
import jax.numpy as jnp
from jax import lax

N = 512
BLOCK = 128
ROW_DEV = 8192
M = 131072
SAMPLES = 2048
SAMP_DEV = 128
N_ROWS = 16


def draw_slab(key, part):
    base_key, column_key = jax.random.split(jax.random.fold_in(key, 11), 2)
    column_scale = jnp.exp(jax.random.uniform(column_key, (1, N), jnp.float32, math.log(0.3), math.log(3.0)))
    base_draw = jax.random.normal(base_key, (M, N), jnp.float32)
    return (base_draw * column_scale).astype(jnp.float32)


def draw_sample_rows(key, part):
    pick_key, high_key = jax.random.split(jax.random.fold_in(key, 23), 2)
    owners = SAMPLES // SAMP_DEV
    row_picks = jax.random.randint(pick_key, (owners, SAMP_DEV), 0, ROW_DEV, dtype=jnp.int32)
    high_slot = jax.random.randint(high_key, (owners, 1), 0, SAMP_DEV, dtype=jnp.int32)
    low_slot = (high_slot + 1) % SAMP_DEV
    slots = jnp.arange(SAMP_DEV, dtype=jnp.int32)[None, :]
    row_picks = jnp.where(slots == high_slot, ROW_DEV - 1, row_picks)
    row_picks = jnp.where(slots == low_slot, 0, row_picks)
    return row_picks.reshape(SAMPLES).astype(jnp.int32)


def with_ends(entries, rng, low, high):
    extent = entries.shape
    index_at = [jax.random.randint(jax.random.fold_in(rng, axis), (), 0, extent[axis]) for axis in range(len(extent))]
    entries = entries.at[tuple(index_at)].set(low)
    longest = extent.index(max(extent))
    index_at[longest] = (index_at[longest] + 1) % extent[longest]
    return entries.at[tuple(index_at)].set(high)


def setup_inputs(seed: int = 0) -> dict:
    streams_of = jax.random.split(jax.random.key(seed), 5)
    return {
        "slab": draw_slab(jax.random.fold_in(streams_of[4], 71), 0),
        "sign_bits": with_ends(jax.random.randint(streams_of[1], (M,), 0, 2), jax.random.fold_in(streams_of[1], 1), 0, 1).astype(jnp.int32),
        "block_mask": with_ends((jax.random.randint(streams_of[2], (M // BLOCK,), 0, 4) < 3).astype(jnp.int32), jax.random.fold_in(streams_of[2], 1), 0, 1),
        "sample_rows": draw_sample_rows(jax.random.fold_in(streams_of[4], 71), 0),
    }


def bit_parity(values, bit_total):
    total = jnp.zeros(values.shape, jnp.int32)
    for position in range(bit_total):
        total = total + jnp.bitwise_and(jnp.right_shift(values, position), 1)
    return jnp.bitwise_and(total, 1)

def sylvester(order_size):
    counter = jnp.arange(order_size, dtype=jnp.int32)
    common = jnp.bitwise_and(counter[:, None], counter[None, :])
    parity = bit_parity(common, max(order_size.bit_length(), 1))
    return (1 - 2 * parity).astype(jnp.float32)

def local_mix(scaled):
    block_count = scaled.shape[0]
    block_rows = scaled.shape[1]
    first_pass = jnp.einsum('jb,rbc->rjc', sylvester(block_rows), scaled, precision=lax.Precision.HIGHEST)
    return jnp.einsum('ir,rjc->ijc', sylvester(block_count), first_pass, precision=lax.Precision.HIGHEST)

def butterfly(values, group_count):
    stride = 1
    while stride < group_count:
        shaped = values.reshape((group_count // (2 * stride), 2, stride) + values.shape[1:])
        lower_half = shaped[:, 0]
        upper_half = shaped[:, 1]
        values = jnp.stack([lower_half + upper_half, lower_half - upper_half], axis=1).reshape(values.shape)
        stride = stride * 2
    return values

def reference(slab, sign_bits, block_mask, sample_rows):
    block_count = ROW_DEV // BLOCK
    sign_values = (2 * sign_bits - 1).astype(jnp.float32)
    mask_values = block_mask.astype(jnp.float32)
    scaled = slab.reshape(N_ROWS, block_count, BLOCK, N) * sign_values.reshape(N_ROWS, block_count, BLOCK, 1)
    scaled = scaled * mask_values.reshape(N_ROWS, block_count, 1, 1)
    mixed_rows = lax.map(local_mix, scaled)
    mixed_rows = butterfly(mixed_rows, N_ROWS).reshape(M, N) * (1.0 / math.sqrt(M))
    owner = jnp.arange(SAMPLES, dtype=jnp.int32) // SAMP_DEV
    global_rows = (owner * ROW_DEV + sample_rows.astype(jnp.int32)).astype(jnp.int32)
    sketch_rows = jnp.take(mixed_rows, global_rows, axis=0)
    gram_matrix = jnp.einsum('sa,sb->ab', sketch_rows, sketch_rows, precision=lax.Precision.HIGHEST) / SAMPLES
    lower_factor = jnp.linalg.cholesky(gram_matrix)
    return (sketch_rows, lower_factor.T)
```

```python
import functools
import math

import jax
import jax.numpy as jnp
from jax import lax
from jax.experimental import pallas as pl
from jax.experimental.pallas import tpu as pltpu
from jax.sharding import PartitionSpec as P

TILE = 256
LANES = 128


def swapped(value, axis, bit):
    return lax.ppermute(value, axis, [(i, i ^ 1 << bit) for i in range(lax.axis_size(axis))])


def parity_sign(common):
    for shift in (16, 8, 4, 2, 1):
        common = common ^ (common >> shift)
    return 1 - 2 * (common & 1)


def butterfly(parts):
    stride = 1
    while stride < len(parts):
        for at in range(len(parts)):
            if at & stride == 0:
                low, high = parts[at], parts[at + stride]
                parts[at], parts[at + stride] = low + high, low - high
        stride *= 2
    return parts


def split_two(value):
    high = value.astype(jnp.bfloat16)
    low = (value - high.astype(jnp.float32)).astype(jnp.bfloat16)
    return high, low


def mix_kernel(mask_ref, pick_ref, slab_ref, sign_ref, send_ref, keep_ref, had_ref, mixed_ref,
               *, inner, outer, pick_count, groups, norm_scale):
    step = pl.program_id(0)
    width = slab_ref.shape[1]

    @pl.when(step == 0)
    def _():
        row = lax.broadcasted_iota(jnp.int32, (TILE, TILE), 0)
        col = lax.broadcasted_iota(jnp.int32, (TILE, TILE), 1)
        had_ref[...] = parity_sign(row & col).astype(jnp.float32).astype(jnp.bfloat16)

    parts = []
    per_tile = TILE // LANES
    for block in range(inner):
        signed = []
        for half in range(per_tile):
            at = block * per_tile + half
            mask = mask_ref[step * inner * per_tile + at]
            sign = (2 * sign_ref[at:at + 1, :] - 1) * mask
            sign = sign.astype(jnp.float32).astype(jnp.bfloat16)
            signed.append(had_ref[:, half * LANES:(half + 1) * LANES] * sign)
        left = jnp.concatenate(signed, axis=1)
        high, low = split_two(slab_ref[block * TILE:(block + 1) * TILE, :])
        mixed = jnp.dot(left, high, preferred_element_type=jnp.float32)
        mixed += jnp.dot(left, low, preferred_element_type=jnp.float32)
        parts.append(mixed)
    parts = butterfly(parts)
    for block in range(inner):
        at = pl.multiple_of((step * inner + block) * TILE, TILE)
        mixed_ref[pl.ds(at, TILE), :] = parts[block]

    @pl.when(step == outer - 1)
    def _():
        span = inner * TILE
        chunk = 8

        @pl.loop(0, span // chunk)
        def _(part):
            base = pl.multiple_of(part * chunk, chunk)
            values = [mixed_ref[pl.ds(base + group * span, chunk), :] for group in range(outer)]
            values = butterfly(values)
            for group in range(outer):
                mixed_ref[pl.ds(base + group * span, chunk), :] = values[group]

        device = lax.axis_index("rows")
        for out_ref, low_bit in ((keep_ref, 0), (send_ref, 1)):
            @pl.loop(0, groups // 2)
            def _(pair):
                owner = device ^ (2 * pair + low_bit)
                scale = parity_sign(owner & device).astype(jnp.float32) * norm_scale
                first = owner * pick_count

                @pl.loop(0, pick_count // 8)
                def _(octet):
                    rows = []
                    for sub in range(8):
                        index = pick_ref[first + octet * 8 + sub]
                        rows.append(mixed_ref[pl.ds(index, 1), :])
                    out_at = pl.multiple_of(pair * pick_count + octet * 8, 8)
                    out_ref[pl.ds(out_at, 8), :] = jnp.concatenate(rows, axis=0) * scale


def mix_and_pick(slab, sign_bits, block_mask, picks, groups):
    row_count, width = slab.shape
    pick_count = picks.shape[0] // groups
    inner = 4
    outer = row_count // (TILE * inner)
    norm_scale = 1.0 / math.sqrt(row_count * groups)
    half = jax.ShapeDtypeStruct((groups // 2 * pick_count, width), jnp.float32)
    span = inner * TILE
    return pl.pallas_call(
        functools.partial(mix_kernel, inner=inner, outer=outer, pick_count=pick_count,
                          groups=groups, norm_scale=norm_scale),
        grid=(outer,),
        in_specs=[
            pl.BlockSpec(memory_space=pltpu.SMEM),
            pl.BlockSpec(memory_space=pltpu.SMEM),
            pl.BlockSpec((span, width), lambda i: (i, 0)),
            pl.BlockSpec((span // LANES, LANES), lambda i: (i, 0)),
        ],
        out_specs=[pl.BlockSpec(half.shape, lambda i: (0, 0))] * 2,
        out_shape=[half, half],
        scratch_shapes=[
            pltpu.VMEM((TILE, TILE), jnp.bfloat16),
            pltpu.VMEM((row_count, width), jnp.float32),
        ],
        compiler_params=pltpu.CompilerParams(
            dimension_semantics=("arbitrary",), vmem_limit_bytes=48 << 20),
    )(block_mask, picks, slab, sign_bits.reshape(row_count // LANES, LANES))


def gather_rows(value, groups):
    device = lax.axis_index("rows")
    for bit in range(groups.bit_length() - 1):
        other = swapped(value, "rows", bit)
        high_bit = (device >> bit) & 1
        value = jnp.where(high_bit == 0, jnp.concatenate([value, other]), jnp.concatenate([other, value]))
    return value


def body(slab, sign_bits, block_mask, sample_rows):
    panel_width = slab.shape[1]
    groups = lax.axis_size("rows")
    bits = groups.bit_length() - 1
    pick_count = sample_rows.shape[0]
    picks = gather_rows(sample_rows, groups)
    send, keep = mix_and_pick(slab, sign_bits, block_mask, picks, groups)
    sketch = keep + swapped(send, "rows", 0)
    for bit in range(1, bits):
        parts = sketch.reshape(-1, 2, pick_count, panel_width)
        sketch = (parts[:, 0] + swapped(parts[:, 1].reshape(-1, panel_width), "rows", bit).reshape(parts[:, 0].shape))
        sketch = sketch.reshape(-1, panel_width)
    full_rows = lax.all_gather(sketch, "cols", axis=1, tiled=True)
    panel_index = lax.axis_index("cols")
    gram_matrix = jnp.einsum("sa,sb->ab", full_rows, full_rows, precision=lax.Precision.HIGHEST)
    for bit in range(bits):
        gram_matrix = gram_matrix + swapped(gram_matrix, "rows", bit)
    gram_matrix = gram_matrix / (pick_count * groups)
    lower_factor = jnp.linalg.cholesky(gram_matrix)
    upper_factor = lower_factor.T
    r_panel = lax.dynamic_slice_in_dim(upper_factor, panel_index * panel_width, panel_width, 1)
    return (sketch, r_panel)


def solution(mesh):
    in_specs = (P("rows", "cols"), P("rows"), P("rows"), P("rows"))
    out_specs = (P("rows", "cols"), P(None, "cols"))
    return jax.shard_map(body, mesh=mesh, in_specs=in_specs, out_specs=out_specs, check_vma=False)
```

```python
import functools
import math

import jax
import jax.numpy as jnp
from jax import lax
from jax.experimental import pallas as pl
from jax.experimental.pallas import tpu as pltpu
from jax.sharding import PartitionSpec as P

TILE = 256
LANES = 128
SUB = 8


def swapped(value, axis, bit):
    return lax.ppermute(value, axis, [(i, i ^ 1 << bit) for i in range(lax.axis_size(axis))])


def parity_sign(common):
    for shift in (16, 8, 4, 2, 1):
        common = common ^ (common >> shift)
    return 1 - 2 * (common & 1)


def butterfly(parts):
    stride = 1
    while stride < len(parts):
        for at in range(len(parts)):
            if at & stride == 0:
                low, high = parts[at], parts[at + stride]
                parts[at], parts[at + stride] = low + high, low - high
        stride *= 2
    return parts


def split_two(value):
    high = value.astype(jnp.bfloat16)
    low = (value - high.astype(jnp.float32)).astype(jnp.bfloat16)
    return high, low


def mix_kernel(mask_ref, pick_ref, slab_ref, sign_ref, keep_ref, send_ref, had_ref, mixed_ref,
               *, inner, outer, pick_count, groups, norm_scale):
    step = pl.program_id(0)
    width = slab_ref.shape[1]

    @pl.when(step == 0)
    def _():
        row = lax.broadcasted_iota(jnp.int32, (TILE, TILE), 0)
        col = lax.broadcasted_iota(jnp.int32, (TILE, TILE), 1)
        had_ref[...] = parity_sign(row & col).astype(jnp.float32).astype(jnp.bfloat16)

    parts = []
    per_tile = TILE // LANES
    for block in range(inner):
        signed = []
        for half in range(per_tile):
            at = block * per_tile + half
            mask = mask_ref[step * inner * per_tile + at]
            sign = (2 * sign_ref[at:at + 1, :] - 1) * mask
            sign = sign.astype(jnp.float32).astype(jnp.bfloat16)
            signed.append(had_ref[:, half * LANES:(half + 1) * LANES] * sign)
        left = jnp.concatenate(signed, axis=1)
        high, low = split_two(slab_ref[block * TILE:(block + 1) * TILE, :])
        mixed = jnp.dot(left, high, preferred_element_type=jnp.float32)
        mixed += jnp.dot(left, low, preferred_element_type=jnp.float32)
        parts.append(mixed)
    parts = butterfly(parts)
    for block in range(inner):
        at = pl.multiple_of((step * inner + block) * TILE, TILE)
        mixed_ref[pl.ds(at, TILE), :] = parts[block]

    @pl.when(step == outer - 1)
    def _():
        span = inner * TILE
        chunk = 8

        @pl.loop(0, span // chunk)
        def _(part):
            base = pl.multiple_of(part * chunk, chunk)
            values = [mixed_ref[pl.ds(base + group * span, chunk), :] for group in range(outer)]
            values = butterfly(values)
            for group in range(outer):
                mixed_ref[pl.ds(base + group * span, chunk), :] = values[group]

        device = lax.axis_index("rows")
        for out_ref, low_bit in ((keep_ref, 0), (send_ref, 1)):
            @pl.loop(0, groups // 2)
            def _(pair):
                owner = device ^ (2 * pair + low_bit)
                scale = parity_sign(owner & device).astype(jnp.float32) * norm_scale
                first = owner * pick_count

                @pl.loop(0, pick_count // 8)
                def _(octet):
                    rows = []
                    for sub in range(8):
                        index = pick_ref[first + octet * 8 + sub]
                        rows.append(mixed_ref[pl.ds(index, 1), :])
                    out_at = pl.multiple_of(pair * pick_count + octet * 8, 8)
                    out_ref[pl.ds(out_at, 8), :] = jnp.concatenate(rows, axis=0) * scale


def mix_and_pick(slab, sign_bits, block_mask, picks, groups):
    row_count, width = slab.shape
    pick_count = picks.shape[0] // groups
    inner = 4
    outer = row_count // (TILE * inner)
    norm_scale = 1.0 / math.sqrt(row_count * groups)
    half = jax.ShapeDtypeStruct((groups // 2 * pick_count, width), jnp.float32)
    span = inner * TILE
    return pl.pallas_call(
        functools.partial(mix_kernel, inner=inner, outer=outer, pick_count=pick_count,
                          groups=groups, norm_scale=norm_scale),
        grid=(outer,),
        in_specs=[
            pl.BlockSpec(memory_space=pltpu.SMEM),
            pl.BlockSpec(memory_space=pltpu.SMEM),
            pl.BlockSpec((span, width), lambda i: (i, 0)),
            pl.BlockSpec((span // LANES, LANES), lambda i: (i, 0)),
        ],
        out_specs=[pl.BlockSpec(half.shape, lambda i: (0, 0))] * 2,
        out_shape=[half, half],
        scratch_shapes=[
            pltpu.VMEM((TILE, TILE), jnp.bfloat16),
            pltpu.VMEM((row_count, width), jnp.float32),
        ],
        compiler_params=pltpu.CompilerParams(
            dimension_semantics=("arbitrary",), vmem_limit_bytes=48 << 20),
    )(block_mask, picks, slab, sign_bits.reshape(row_count // LANES, LANES))


def gram_kernel(full_ref, keep_ref, send_ref, gram_ref, *, strips, scale):
    total = full_ref.shape[1]
    height = LANES // strips
    mine = lax.axis_index("rows") & (strips - 1)
    block = 0
    for upper in range(total // LANES):
        left = full_ref[:, upper * LANES:(upper + 1) * LANES]
        rows = lax.dot_general(left, full_ref[:, upper * LANES:], (((0,), (0,)), ((), ())),
                               precision=lax.Precision.HIGHEST, preferred_element_type=jnp.float32)
        gram_ref[:, :total - upper * LANES] = rows * scale
        for right in range(upper, total // LANES):
            at = (right - upper) * LANES
            for low_bit, out_ref in ((0, keep_ref), (1, send_ref)):
                for half in range(strips // 2):
                    strip = pl.multiple_of(((low_bit + 2 * half) ^ mine) * height, height)
                    out_ref[half, block * height:(block + 1) * height, :] = gram_ref[
                        pl.ds(strip, height), at:at + LANES]
            block += 1


def partial_gram(full_rows, strips, scale):
    total = full_rows.shape[1]
    tiles = total // LANES
    half = jax.ShapeDtypeStruct(
        (strips // 2, tiles * (tiles + 1) // 2 * (LANES // strips), LANES), jnp.float32)
    return pl.pallas_call(
        functools.partial(gram_kernel, strips=strips, scale=scale),
        out_shape=[half, half],
        scratch_shapes=[pltpu.VMEM((LANES, total), jnp.float32)],
        compiler_params=pltpu.CompilerParams(vmem_limit_bytes=48 << 20),
    )(full_rows)


def lane_splat(value, lane):
    return jnp.broadcast_to(value[:, lane:lane + 1], (value.shape[0], LANES))


def row_splat(value, row):
    return jnp.broadcast_to(value[row:row + 1, :], value.shape)


def factor_tile(tile):
    done = []
    copies = tile[0].shape[1] // LANES
    sub_row = lax.broadcasted_iota(jnp.int32, tile[0].shape, 0)

    def widen(value):
        return jnp.concatenate([value] * copies, axis=1)

    for at in range(len(tile)):
        lead = tile[at]
        columns = [lane_splat(lead[:, :LANES], SUB * at + j) for j in range(SUB)]
        pivot = {(i, j): row_splat(columns[j], i) for j in range(SUB) for i in range(j + 1)}
        below = [[lane_splat(tile[u][:, :LANES], SUB * at + j) for j in range(SUB)]
                 for u in range(at + 1, len(tile))]
        rows = [row_splat(lead, m) for m in range(SUB)]
        panel = jnp.zeros_like(lead)
        for m in range(SUB):
            inverse = lax.rsqrt(pivot[m, m])
            for j in range(m + 1, SUB):
                pivot[m, j] = pivot[m, j] * inverse
            for i in range(m + 1, SUB):
                for j in range(i, SUB):
                    pivot[i, j] = pivot[i, j] - pivot[m, i] * pivot[m, j]
            rows[m] = rows[m] * widen(inverse)
            for j in range(m + 1, SUB):
                rows[j] = rows[j] - widen(pivot[m, j]) * rows[m]
            panel = jnp.where(sub_row == m, rows[m], panel)
            for u, column in enumerate(below):
                column[m] = column[m] * inverse
                for j in range(m + 1, SUB):
                    column[j] = column[j] - pivot[m, j] * column[m]
                tile[at + 1 + u] = tile[at + 1 + u] - widen(column[m]) * rows[m]
        done.append(panel)
    return done


def factor_kernel(even_ref, odd_ref, out_ref, gram_ref, factor_ref, *, strips):
    total = gram_ref.shape[0]
    tiles = total // LANES
    height = LANES // strips
    mine = lax.axis_index("rows") & (strips - 1)
    block = 0
    for upper in range(tiles):
        for right in range(upper, tiles):
            for low_bit, in_ref in ((0, even_ref), (1, odd_ref)):
                for half in range(strips // 2):
                    strip = pl.multiple_of(((low_bit + 2 * half) ^ mine) * height, height)
                    gram_ref[pl.ds(upper * LANES + strip, height), right * LANES:(right + 1) * LANES] = in_ref[
                        half, block * height:(block + 1) * height, :]
            block += 1
    factor_ref[...] = jnp.zeros_like(factor_ref)
    row = lax.broadcasted_iota(jnp.int32, (LANES, LANES), 0)
    col = lax.broadcasted_iota(jnp.int32, (LANES, LANES), 1)
    identity = (row == col).astype(jnp.float32)
    for at in range(tiles):
        here = slice(at * LANES, (at + 1) * LANES)
        diagonal = jnp.concatenate([gram_ref[here, here], identity], axis=1)
        slabs = [diagonal[SUB * t:SUB * t + SUB] for t in range(LANES // SUB)]
        factored = jnp.concatenate(factor_tile(slabs), axis=0)
        factor_ref[here, here] = jnp.where(col >= row, factored[:, :LANES], 0.0)
        if at < tiles - 1:
            rest = (at + 1) * LANES
            panel = jnp.dot(factored[:, LANES:], gram_ref[here, rest:], precision=lax.Precision.HIGHEST,
                            preferred_element_type=jnp.float32)
            factor_ref[here, rest:] = panel
            for below in range(at + 1, tiles):
                skip = (below - at - 1) * LANES
                gram_ref[below * LANES:(below + 1) * LANES, below * LANES:] -= lax.dot_general(
                    panel[:, skip:skip + LANES], panel[:, skip:], (((0,), (0,)), ((), ())),
                    precision=lax.Precision.HIGHEST, preferred_element_type=jnp.float32)
    width = out_ref.shape[1]
    first = pl.multiple_of(lax.axis_index("cols") * width, width)
    out_ref[...] = factor_ref[:, pl.ds(first, width)]


def factor_panel(even, odd, total, width):
    strips = 2 * even.shape[0]
    return pl.pallas_call(
        functools.partial(factor_kernel, strips=strips),
        out_shape=jax.ShapeDtypeStruct((total, width), jnp.float32),
        scratch_shapes=[pltpu.VMEM((total, total), jnp.float32)] * 2,
        compiler_params=pltpu.CompilerParams(vmem_limit_bytes=48 << 20),
    )(even, odd)


def gather_rows(value, groups):
    device = lax.axis_index("rows")
    for bit in range(groups.bit_length() - 1):
        other = swapped(value, "rows", bit)
        high_bit = (device >> bit) & 1
        value = jnp.where(high_bit == 0, jnp.concatenate([value, other]), jnp.concatenate([other, value]))
    return value


def body(slab, sign_bits, block_mask, sample_rows):
    panel_width = slab.shape[1]
    groups = lax.axis_size("rows")
    bits = groups.bit_length() - 1
    pick_count = sample_rows.shape[0]
    picks = gather_rows(sample_rows, groups)
    keep, send = mix_and_pick(slab, sign_bits, block_mask, picks, groups)
    sketch = keep + swapped(send, "rows", 0)
    for bit in range(1, bits):
        parts = sketch.reshape(-1, 2, pick_count, panel_width)
        sketch = (parts[:, 0] + swapped(parts[:, 1].reshape(-1, panel_width), "rows", bit).reshape(parts[:, 0].shape))
        sketch = sketch.reshape(-1, panel_width)
    full_rows = lax.all_gather(sketch, "cols", axis=1, tiled=True)
    keep, send = partial_gram(full_rows, 4, 1.0 / (pick_count * groups))
    gram = keep + swapped(send, "rows", 0)
    gram = gram[:1] + swapped(gram[1:], "rows", 1)
    for bit in range(2, bits):
        gram = gram + swapped(gram, "rows", bit)
    gram = jnp.concatenate([gram, swapped(gram, "rows", 1)])
    r_panel = factor_panel(gram, swapped(gram, "rows", 0), full_rows.shape[1], panel_width)
    return (sketch, r_panel)


def solution(mesh):
    in_specs = (P("rows", "cols"), P("rows"), P("rows"), P("rows"))
    out_specs = (P("rows", "cols"), P(None, "cols"))
    return jax.shard_map(body, mesh=mesh, in_specs=in_specs, out_specs=out_specs, check_vma=False)
```

```python
import functools
import math

import jax
import jax.numpy as jnp
from jax import lax
from jax.experimental import pallas as pl
from jax.experimental.pallas import tpu as pltpu
from jax.sharding import PartitionSpec as P

TILE = 256
LANES = 128
SUB = 8


def swapped(value, axis, bit):
    return lax.ppermute(value, axis, [(i, i ^ 1 << bit) for i in range(lax.axis_size(axis))])


def parity_sign(common):
    for shift in (16, 8, 4, 2, 1):
        common = common ^ (common >> shift)
    return 1 - 2 * (common & 1)


def butterfly(parts):
    stride = 1
    while stride < len(parts):
        for at in range(len(parts)):
            if at & stride == 0:
                low, high = parts[at], parts[at + stride]
                parts[at], parts[at + stride] = low + high, low - high
        stride *= 2
    return parts


def split_two(value):
    high = value.astype(jnp.bfloat16)
    low = (value - high.astype(jnp.float32)).astype(jnp.bfloat16)
    return high, low


def mix_kernel(slab_ref, sign_ref, mask_ref, *refs, first, earlier):
    joined = refs[:earlier]
    out_ref, had_ref, buf_ref, bits_ref, flags_ref, sems = refs[earlier:]
    rows = buf_ref.shape[0]
    chunks = sems.shape[0] - 2
    span = rows // chunks
    per_tile = TILE // LANES

    def fetch(part):
        return pltpu.make_async_copy(slab_ref.at[pl.ds(first + part * span, span), :],
                                     buf_ref.at[pl.ds(part * span, span), :], sems.at[part])

    bits_copy = pltpu.make_async_copy(sign_ref, bits_ref, sems.at[chunks])
    flags_copy = pltpu.make_async_copy(mask_ref, flags_ref, sems.at[chunks + 1])
    bits_copy.start()
    flags_copy.start()
    for part in range(chunks):
        fetch(part).start()
    row = lax.broadcasted_iota(jnp.int32, (TILE, TILE), 0)
    col = lax.broadcasted_iota(jnp.int32, (TILE, TILE), 1)
    had_ref[...] = parity_sign(row & col).astype(jnp.float32).astype(jnp.bfloat16)
    bits_copy.wait()
    flags_copy.wait()
    base_out = out_ref.shape[0] - rows
    tiles = span // TILE
    for part in range(chunks):
        fetch(part).wait()
        mixed = []
        for block in range(part * tiles, (part + 1) * tiles):
            signed = []
            for half in range(per_tile):
                at = first // LANES + block * per_tile + half
                sign = (2 * bits_ref[at:at + 1, :] - 1) * flags_ref[at]
                sign = sign.astype(jnp.float32).astype(jnp.bfloat16)
                signed.append(had_ref[:, half * LANES:(half + 1) * LANES] * sign)
            left = jnp.concatenate(signed * 2, axis=1)
            right = jnp.concatenate(split_two(buf_ref[block * TILE:(block + 1) * TILE, :]), axis=0)
            mixed.append(jnp.dot(left, right, preferred_element_type=jnp.float32))
        mixed = butterfly(mixed)
        for block in range(tiles):
            at = base_out + (part * tiles + block) * TILE
            out_ref[at:at + TILE, :] = mixed[block]

    @pl.loop(0, span // SUB // 4)
    def _(part):
        for eighth in range(4):
            base = pl.multiple_of(part * 4 * SUB, 4 * SUB) + eighth * SUB
            values = butterfly([out_ref[pl.ds(base_out + base + at * span, SUB), :] for at in range(chunks)])
            for at in range(chunks):
                out_ref[pl.ds(base_out + base + at * span, SUB), :] = values[at]

    if earlier:
        @pl.loop(0, rows // SUB // 8)
        def _(part):
            for eighth in range(8):
                base = pl.multiple_of(part * 8 * SUB, 8 * SUB) + eighth * SUB
                values = [ref[pl.ds(base, SUB), :] for ref in joined]
                values = butterfly(values + [out_ref[pl.ds(base_out + base, SUB), :]])
                for at in range(earlier + 1):
                    out_ref[pl.ds(base + at * rows, SUB), :] = values[at]


def mix_run(slab, sign_bits, block_mask, first, rows, earlier):
    width = slab.shape[1]
    chunks = 4
    flags = block_mask.shape[0]
    held = rows * (len(earlier) + 1)
    return pl.pallas_call(
        functools.partial(mix_kernel, first=first, earlier=len(earlier)),
        in_specs=[pl.BlockSpec(memory_space=pltpu.HBM)] * 3 + [pl.BlockSpec(memory_space=pltpu.VMEM)] * len(earlier),
        out_specs=pl.BlockSpec(memory_space=pltpu.VMEM),
        out_shape=jax.ShapeDtypeStruct((held, width), jnp.float32),
        scratch_shapes=[
            pltpu.VMEM((TILE, TILE), jnp.bfloat16),
            pltpu.VMEM((rows, width), jnp.float32),
            pltpu.VMEM((flags, LANES), jnp.int32),
            pltpu.SMEM((flags,), jnp.int32),
            pltpu.SemaphoreType.DMA((chunks + 2,)),
        ],
        compiler_params=pltpu.CompilerParams(vmem_limit_bytes=(36 if earlier else 50) << 20),
    )(slab, sign_bits, block_mask, *earlier)


def pick_kernel(pick_ref, mixed_ref, keep_ref, send_ref, *, start, count, order, pick_count, groups, norm_scale):
    device = lax.axis_index("rows")
    sub_row = lax.broadcasted_iota(jnp.int32, (SUB, mixed_ref.shape[1]), 0)
    octets = count // SUB
    for out_ref, low_bit in ((send_ref, 1), (keep_ref, 0)):
        @pl.loop(0, groups // 2)
        def _(pair):
            offset = low_bit
            for place, bit in enumerate(reversed(order)):
                offset = offset | ((pair >> place) & 1) << bit
            scale = parity_sign((device ^ offset) & device).astype(jnp.float32) * norm_scale
            for octet in range(octets):
                rows = None
                for sub in range(SUB):
                    index = pick_ref[offset * pick_count + start + octet * SUB + sub]
                    taken = jnp.broadcast_to(mixed_ref[pl.ds(index, 1), :], sub_row.shape)
                    rows = taken if rows is None else jnp.where(sub_row == sub, taken, rows)
                out_at = pl.multiple_of(pair * count + octet * SUB, SUB)
                out_ref[pl.ds(out_at, SUB), :] = rows * scale


def pick_rows(picks, mixed, start, count, order, groups):
    norm_scale = 1.0 / math.sqrt(mixed.shape[0] * groups)
    half = jax.ShapeDtypeStruct((groups // 2 * count, mixed.shape[1]), jnp.float32)
    return pl.pallas_call(
        functools.partial(pick_kernel, start=start, count=count, order=order, pick_count=picks.shape[0] // groups,
                          groups=groups, norm_scale=norm_scale),
        in_specs=[pl.BlockSpec(memory_space=pltpu.SMEM), pl.BlockSpec(memory_space=pltpu.VMEM)],
        out_specs=[pl.BlockSpec(memory_space=pltpu.VMEM)] * 2,
        out_shape=[half, half],
        compiler_params=pltpu.CompilerParams(vmem_limit_bytes=32 << 20),
    )(picks, mixed)


def gram_kernel(*refs, strips, scale, peers):
    pieces, (keep_ref, send_ref, full_ref, gram_ref) = refs[:-4], refs[-4:]
    total = full_ref.shape[1]
    width = total // peers
    column = lax.axis_index("cols")
    at = 0
    for run in range(len(pieces) // peers):
        count = pieces[run * peers].shape[0]
        for peer in range(peers):
            first = pl.multiple_of((column ^ peer) * width, width)
            full_ref[at:at + count, pl.ds(first, width)] = pieces[run * peers + peer][...]
        at += count
    height = LANES // strips
    mine = lax.axis_index("rows") & (strips - 1)
    block = 0
    for upper in range(total // LANES):
        left = full_ref[:, upper * LANES:(upper + 1) * LANES]
        rows = lax.dot_general(left, full_ref[:, upper * LANES:], (((0,), (0,)), ((), ())),
                               precision=lax.Precision.HIGHEST, preferred_element_type=jnp.float32)
        gram_ref[:, :total - upper * LANES] = rows * scale
        for right in range(upper, total // LANES):
            lane = (right - upper) * LANES
            for low_bit, out_ref in ((0, keep_ref), (1, send_ref)):
                for half in range(strips // 2):
                    strip = pl.multiple_of(((low_bit + 2 * half) ^ mine) * height, height)
                    out_ref[half, block * height:(block + 1) * height, :] = gram_ref[
                        pl.ds(strip, height), lane:lane + LANES]
            block += 1


def partial_gram(pieces, rows, peers, strips, scale):
    total = pieces[0].shape[1] * peers
    tiles = total // LANES
    half = jax.ShapeDtypeStruct(
        (strips // 2, tiles * (tiles + 1) // 2 * (LANES // strips), LANES), jnp.float32)
    return pl.pallas_call(
        functools.partial(gram_kernel, strips=strips, scale=scale, peers=peers),
        out_shape=[half, half],
        scratch_shapes=[pltpu.VMEM((rows, total), jnp.float32), pltpu.VMEM((LANES, total), jnp.float32)],
        compiler_params=pltpu.CompilerParams(vmem_limit_bytes=16 << 20),
    )(*pieces)


def lane_splat(value, lane):
    return jnp.broadcast_to(value[:, lane:lane + 1], (value.shape[0], LANES))


def row_splat(value, row):
    return jnp.broadcast_to(value[row:row + 1, :], value.shape)


def factor_tile(tile):
    done = []
    copies = tile[0].shape[1] // LANES
    sub_row = lax.broadcasted_iota(jnp.int32, tile[0].shape, 0)

    def widen(value):
        return jnp.concatenate([value] * copies, axis=1)

    for at in range(len(tile)):
        lead = tile[at]
        columns = [lane_splat(lead[:, :LANES], SUB * at + j) for j in range(SUB)]
        pivot = {(i, j): row_splat(columns[j], i) for j in range(SUB) for i in range(j + 1)}
        below = [[lane_splat(tile[u][:, :LANES], SUB * at + j) for j in range(SUB)]
                 for u in range(at + 1, len(tile))]
        rows = [row_splat(lead, m) for m in range(SUB)]
        panel = jnp.zeros_like(lead)
        for m in range(SUB):
            inverse = lax.rsqrt(pivot[m, m])
            for j in range(m + 1, SUB):
                pivot[m, j] = pivot[m, j] * inverse
            for i in range(m + 1, SUB):
                for j in range(i, SUB):
                    pivot[i, j] = pivot[i, j] - pivot[m, i] * pivot[m, j]
            rows[m] = rows[m] * widen(inverse)
            for j in range(m + 1, SUB):
                rows[j] = rows[j] - widen(pivot[m, j]) * rows[m]
            panel = jnp.where(sub_row == m, rows[m], panel)
            for u, column in enumerate(below):
                column[m] = column[m] * inverse
                for j in range(m + 1, SUB):
                    column[j] = column[j] - pivot[m, j] * column[m]
                tile[at + 1 + u] = tile[at + 1 + u] - widen(column[m]) * rows[m]
        done.append(panel)
    return done


def factor_kernel(even_ref, odd_ref, out_ref, gram_ref, factor_ref, *, strips):
    total = gram_ref.shape[0]
    tiles = total // LANES
    height = LANES // strips
    mine = lax.axis_index("rows") & (strips - 1)
    block = 0
    for upper in range(tiles):
        for right in range(upper, tiles):
            for low_bit, in_ref in ((0, even_ref), (1, odd_ref)):
                for half in range(strips // 2):
                    strip = pl.multiple_of(((low_bit + 2 * half) ^ mine) * height, height)
                    gram_ref[pl.ds(upper * LANES + strip, height), right * LANES:(right + 1) * LANES] = in_ref[
                        half, block * height:(block + 1) * height, :]
            block += 1
    factor_ref[...] = jnp.zeros_like(factor_ref)
    row = lax.broadcasted_iota(jnp.int32, (LANES, LANES), 0)
    col = lax.broadcasted_iota(jnp.int32, (LANES, LANES), 1)
    identity = (row == col).astype(jnp.float32)
    for at in range(tiles):
        here = slice(at * LANES, (at + 1) * LANES)
        diagonal = jnp.concatenate([gram_ref[here, here], identity], axis=1)
        slabs = [diagonal[SUB * t:SUB * t + SUB] for t in range(LANES // SUB)]
        factored = jnp.concatenate(factor_tile(slabs), axis=0)
        factor_ref[here, here] = jnp.where(col >= row, factored[:, :LANES], 0.0)
        if at < tiles - 1:
            rest = (at + 1) * LANES
            panel = jnp.dot(factored[:, LANES:], gram_ref[here, rest:], precision=lax.Precision.HIGHEST,
                            preferred_element_type=jnp.float32)
            factor_ref[here, rest:] = panel
            for below in range(at + 1, tiles):
                skip = (below - at - 1) * LANES
                gram_ref[below * LANES:(below + 1) * LANES, below * LANES:] -= lax.dot_general(
                    panel[:, skip:skip + LANES], panel[:, skip:], (((0,), (0,)), ((), ())),
                    precision=lax.Precision.HIGHEST, preferred_element_type=jnp.float32)
    width = out_ref.shape[1]
    first = pl.multiple_of(lax.axis_index("cols") * width, width)
    out_ref[...] = factor_ref[:, pl.ds(first, width)]


def factor_panel(even, odd, total, width):
    strips = 2 * even.shape[0]
    return pl.pallas_call(
        functools.partial(factor_kernel, strips=strips),
        out_shape=jax.ShapeDtypeStruct((total, width), jnp.float32),
        scratch_shapes=[pltpu.VMEM((total, total), jnp.float32)] * 2,
        compiler_params=pltpu.CompilerParams(vmem_limit_bytes=48 << 20),
    )(even, odd)


def reduce_run(keep, send, order):
    value = keep + swapped(send, "rows", 0)
    for bit in order:
        half = value.shape[0] // 2
        value = value[:half] + swapped(value[half:], "rows", bit)
    return value


def body(slab, sign_bits, block_mask, sample_rows):
    row_count, panel_width = slab.shape
    groups = lax.axis_size("rows")
    peers = lax.axis_size("cols")
    bits = groups.bit_length() - 1
    pick_count = sample_rows.shape[0]
    signs = sign_bits.reshape(row_count // LANES, LANES)
    picks = sample_rows
    runs = 4
    rows = row_count // runs
    mixed = []
    source = slab
    for bit in range(bits):
        other = swapped(picks, "rows", bit)
        run = bit - (bits - runs)
        if run >= 0:
            made = mix_run(source, signs, block_mask, run * rows, rows, mixed if run == runs - 1 else [])
            other, made, source = lax.optimization_barrier((other, made, source))
            mixed.append(made)
        picks = jnp.concatenate([picks, other])
    mixed = mixed[-1]
    first = pick_count // 2
    cross = list(range(1, bits))
    sketch = []
    pieces = []
    for start, count, order in ((0, first, cross), (first, pick_count - first, cross[1:] + cross[:1])):
        keep, send = pick_rows(picks, mixed, start, count, order, groups)
        part = reduce_run(keep, send, order)
        sketch.append(part)
        pieces.append(part)
        for peer in range(1, peers):
            pieces.append(lax.ppermute(part, "cols", [(i, i ^ peer) for i in range(peers)]))
    sketch = jnp.concatenate(sketch)
    keep, send = partial_gram(pieces, pick_count, peers, 4, 1.0 / (pick_count * groups))
    gram = keep + swapped(send, "rows", 0)
    gram = gram[:1] + swapped(gram[1:], "rows", 1)
    for bit in range(2, bits):
        gram = gram + swapped(gram, "rows", bit)
    gram = jnp.concatenate([gram, swapped(gram, "rows", 1)])
    r_panel = factor_panel(gram, swapped(gram, "rows", 0), panel_width * peers, panel_width)
    return (sketch, r_panel)


def solution(mesh):
    in_specs = (P("rows", "cols"), P("rows"), P("rows"), P("rows"))
    out_specs = (P("rows", "cols"), P(None, "cols"))
    return jax.shard_map(body, mesh=mesh, in_specs=in_specs, out_specs=out_specs, check_vma=False)
```

```python
import functools
import math

import jax
import jax.numpy as jnp
from jax import lax
from jax.experimental import pallas as pl
from jax.experimental.pallas import tpu as pltpu
from jax.sharding import PartitionSpec as P

TILE = 256
LANES = 128
SUB = 8
AHEAD = 3


def swapped(value, axis, bit):
    return lax.ppermute(value, axis, [(i, i ^ 1 << bit) for i in range(lax.axis_size(axis))])


def parity_sign(common):
    for shift in (16, 8, 4, 2, 1):
        common = common ^ (common >> shift)
    return 1 - 2 * (common & 1)


def butterfly(parts):
    stride = 1
    while stride < len(parts):
        for at in range(len(parts)):
            if at & stride == 0:
                low, high = parts[at], parts[at + stride]
                parts[at], parts[at + stride] = low + high, low - high
        stride *= 2
    return parts


def split_two(value):
    high = value.astype(jnp.bfloat16)
    low = (value - high.astype(jnp.float32)).astype(jnp.bfloat16)
    return high, low


def mix_kernel(slab_ref, sign_ref, mask_ref, *refs, first, earlier):
    joined = refs[:earlier]
    out_ref, had_ref, buf_ref, bits_ref, flags_ref, sems = refs[earlier:]
    rows = buf_ref.shape[0]
    chunks = sems.shape[0] - 2
    span = rows // chunks
    per_tile = TILE // LANES

    def fetch(part):
        return pltpu.make_async_copy(slab_ref.at[pl.ds(first + part * span, span), :],
                                     buf_ref.at[pl.ds(part * span, span), :], sems.at[part])

    bits_copy = pltpu.make_async_copy(sign_ref, bits_ref, sems.at[chunks])
    flags_copy = pltpu.make_async_copy(mask_ref, flags_ref, sems.at[chunks + 1])
    bits_copy.start()
    flags_copy.start()
    for part in range(chunks):
        fetch(part).start()
    row = lax.broadcasted_iota(jnp.int32, (TILE, TILE), 0)
    col = lax.broadcasted_iota(jnp.int32, (TILE, TILE), 1)
    had_ref[...] = parity_sign(row & col).astype(jnp.float32).astype(jnp.bfloat16)
    bits_copy.wait()
    flags_copy.wait()
    base_out = out_ref.shape[0] - rows
    tiles = span // TILE
    for part in range(chunks):
        fetch(part).wait()
        mixed = []
        for block in range(part * tiles, (part + 1) * tiles):
            signed = []
            for half in range(per_tile):
                at = first // LANES + block * per_tile + half
                sign = (2 * bits_ref[at:at + 1, :] - 1) * flags_ref[at]
                sign = sign.astype(jnp.float32).astype(jnp.bfloat16)
                signed.append(had_ref[:, half * LANES:(half + 1) * LANES] * sign)
            left = jnp.concatenate(signed * 2, axis=1)
            right = jnp.concatenate(split_two(buf_ref[block * TILE:(block + 1) * TILE, :]), axis=0)
            mixed.append(jnp.dot(left, right, preferred_element_type=jnp.float32))
        mixed = butterfly(mixed)
        for block in range(tiles):
            at = base_out + (part * tiles + block) * TILE
            out_ref[at:at + TILE, :] = mixed[block]

    @pl.loop(0, span // SUB // 4)
    def _(part):
        for eighth in range(4):
            base = pl.multiple_of(part * 4 * SUB, 4 * SUB) + eighth * SUB
            values = butterfly([out_ref[pl.ds(base_out + base + at * span, SUB), :] for at in range(chunks)])
            for at in range(chunks):
                out_ref[pl.ds(base_out + base + at * span, SUB), :] = values[at]

    if earlier:
        @pl.loop(0, rows // SUB // 8)
        def _(part):
            for eighth in range(8):
                base = pl.multiple_of(part * 8 * SUB, 8 * SUB) + eighth * SUB
                values = [ref[pl.ds(base, SUB), :] for ref in joined]
                values = butterfly(values + [out_ref[pl.ds(base_out + base, SUB), :]])
                for at in range(earlier + 1):
                    out_ref[pl.ds(base + at * rows, SUB), :] = values[at]


def mix_run(slab, sign_bits, block_mask, first, rows, earlier):
    width = slab.shape[1]
    chunks = 4
    flags = block_mask.shape[0]
    held = rows * (len(earlier) + 1)
    return pl.pallas_call(
        functools.partial(mix_kernel, first=first, earlier=len(earlier)),
        in_specs=[pl.BlockSpec(memory_space=pltpu.HBM)] * 3 + [pl.BlockSpec(memory_space=pltpu.VMEM)] * len(earlier),
        out_specs=pl.BlockSpec(memory_space=pltpu.VMEM),
        out_shape=jax.ShapeDtypeStruct((held, width), jnp.float32),
        scratch_shapes=[
            pltpu.VMEM((TILE, TILE), jnp.bfloat16),
            pltpu.VMEM((rows, width), jnp.float32),
            pltpu.VMEM((flags, LANES), jnp.int32),
            pltpu.SMEM((flags,), jnp.int32),
            pltpu.SemaphoreType.DMA((chunks + 2,)),
        ],
        compiler_params=pltpu.CompilerParams(vmem_limit_bytes=(36 if earlier else 50) << 20),
    )(slab, sign_bits, block_mask, *earlier)


def pick_kernel(pick_ref, mixed_ref, keep_ref, send_ref, *, start, count, order, pick_count, groups, norm_scale):
    device = lax.axis_index("rows")
    sub_row = lax.broadcasted_iota(jnp.int32, (SUB, mixed_ref.shape[1]), 0)
    octets = count // SUB
    for out_ref, low_bit in ((send_ref, 1), (keep_ref, 0)):
        @pl.loop(0, groups // 2)
        def _(pair):
            offset = low_bit
            for place, bit in enumerate(reversed(order)):
                offset = offset | ((pair >> place) & 1) << bit
            scale = parity_sign((device ^ offset) & device).astype(jnp.float32) * norm_scale
            for octet in range(octets):
                rows = None
                for sub in range(SUB):
                    index = pick_ref[offset * pick_count + start + octet * SUB + sub]
                    taken = jnp.broadcast_to(mixed_ref[pl.ds(index, 1), :], sub_row.shape)
                    rows = taken if rows is None else jnp.where(sub_row == sub, taken, rows)
                out_at = pl.multiple_of(pair * count + octet * SUB, SUB)
                out_ref[pl.ds(out_at, SUB), :] = rows * scale


def pick_rows(picks, mixed, start, count, order, groups):
    norm_scale = 1.0 / math.sqrt(mixed.shape[0] * groups)
    half = jax.ShapeDtypeStruct((groups // 2 * count, mixed.shape[1]), jnp.float32)
    return pl.pallas_call(
        functools.partial(pick_kernel, start=start, count=count, order=order, pick_count=picks.shape[0] // groups,
                          groups=groups, norm_scale=norm_scale),
        in_specs=[pl.BlockSpec(memory_space=pltpu.SMEM), pl.BlockSpec(memory_space=pltpu.VMEM)],
        out_specs=[pl.BlockSpec(memory_space=pltpu.VMEM)] * 2,
        out_shape=[half, half],
        compiler_params=pltpu.CompilerParams(vmem_limit_bytes=32 << 20),
    )(picks, mixed)


def gram_kernel(*refs, strips, scale, peers):
    pieces, (keep_ref, send_ref, full_ref, gram_ref) = refs[:-4], refs[-4:]
    total = full_ref.shape[1]
    width = total // peers
    column = lax.axis_index("cols")
    at = 0
    for run in range(len(pieces) // peers):
        count = pieces[run * peers].shape[0]
        for peer in range(peers):
            first = pl.multiple_of((column ^ peer) * width, width)
            full_ref[at:at + count, pl.ds(first, width)] = pieces[run * peers + peer][...]
        at += count
    height = LANES // strips
    mine = lax.axis_index("rows") & (strips - 1)
    block = 0
    for upper in range(total // LANES):
        left = full_ref[:, upper * LANES:(upper + 1) * LANES]
        rows = lax.dot_general(left, full_ref[:, upper * LANES:], (((0,), (0,)), ((), ())),
                               precision=lax.Precision.HIGHEST, preferred_element_type=jnp.float32)
        gram_ref[:, :total - upper * LANES] = rows * scale
        for right in range(upper, total // LANES):
            lane = (right - upper) * LANES
            for low_bit, out_ref in ((0, keep_ref), (1, send_ref)):
                for half in range(strips // 2):
                    strip = pl.multiple_of(((low_bit + 2 * half) ^ mine) * height, height)
                    out_ref[half, block * height:(block + 1) * height, :] = gram_ref[
                        pl.ds(strip, height), lane:lane + LANES]
            block += 1


def partial_gram(pieces, rows, peers, strips, scale):
    total = pieces[0].shape[1] * peers
    tiles = total // LANES
    half = jax.ShapeDtypeStruct(
        (strips // 2, tiles * (tiles + 1) // 2 * (LANES // strips), LANES), jnp.float32)
    return pl.pallas_call(
        functools.partial(gram_kernel, strips=strips, scale=scale, peers=peers),
        out_shape=[half, half],
        scratch_shapes=[pltpu.VMEM((rows, total), jnp.float32), pltpu.VMEM((LANES, total), jnp.float32)],
        compiler_params=pltpu.CompilerParams(vmem_limit_bytes=16 << 20),
    )(*pieces)


def split_three(value):
    high = value.astype(jnp.bfloat16).astype(jnp.float32)
    rest = value - high
    middle = rest.astype(jnp.bfloat16).astype(jnp.float32)
    return high, middle, rest - middle


def left_terms(value, axis):
    high, middle, low = split_three(value)
    return jnp.concatenate([high, high, middle, high, middle, low], axis=axis).astype(jnp.bfloat16)


def right_terms(value):
    high, middle, low = split_three(value)
    return jnp.concatenate([high, middle, high, low, middle, high], axis=0).astype(jnp.bfloat16)


def times(left, right):
    return jnp.dot(left_terms(left, 1), right_terms(right), preferred_element_type=jnp.float32)


def inner_product(left, right):
    return lax.dot_general(left_terms(left, 0), right_terms(right), (((0,), (0,)), ((), ())),
                           preferred_element_type=jnp.float32)


def lane_splat(value, lane):
    return jnp.broadcast_to(value[:, lane:lane + 1], (value.shape[0], LANES))


def factor_tile(diagonal, column_ref, lead_ref):
    row = lax.broadcasted_iota(jnp.int32, (LANES, LANES), 0)
    col = lax.broadcasted_iota(jnp.int32, (LANES, LANES), 1)
    identity = (row == col).astype(jnp.float32)
    whole = jnp.concatenate([diagonal, identity], axis=1)
    slabs = LANES // SUB
    tile = [whole[SUB * t:SUB * t + SUB] for t in range(slabs)]
    sub_row = lax.broadcasted_iota(jnp.int32, tile[0].shape, 0)
    done = []

    def widen(value):
        return jnp.concatenate([value, value], axis=1)

    for at in range(slabs):
        lead = tile[at]
        direct = range(at + 1, min(slabs, at + 1 + AHEAD))
        for j in range(SUB):
            column_ref[(at * SUB + j) * SUB:(at * SUB + j + 1) * SUB, :] = lane_splat(lead[:, :LANES], SUB * at + j)
        for half in range(2):
            lead_ref[half * LANES + at * SUB:half * LANES + (at + 1) * SUB, :] = lead[:, half * LANES:(half + 1) * LANES]
        pivot = {(i, j): column_ref[pl.ds((at * SUB + j) * SUB + i, SUB, stride=0), :]
                 for j in range(SUB) for i in range(j + 1)}
        below = [[lane_splat(tile[u][:, :LANES], SUB * at + j) for j in range(SUB)] for u in direct]
        rows = [jnp.concatenate([lead_ref[pl.ds(half * LANES + at * SUB + m, SUB, stride=0), :] for half in range(2)],
                                axis=1) for m in range(SUB)]
        panel = jnp.zeros_like(lead)
        for m in range(SUB):
            inverse = lax.rsqrt(pivot[m, m])
            for j in range(m + 1, SUB):
                pivot[m, j] = pivot[m, j] * inverse
            for i in range(m + 1, SUB):
                for j in range(i, SUB):
                    pivot[i, j] = pivot[i, j] - pivot[m, i] * pivot[m, j]
            rows[m] = rows[m] * widen(inverse)
            for j in range(m + 1, SUB):
                rows[j] = rows[j] - widen(pivot[m, j]) * rows[m]
            panel = jnp.where(sub_row == m, rows[m], panel)
            for column, u in zip(below, direct):
                column[m] = column[m] * inverse
                for j in range(m + 1, SUB):
                    column[j] = column[j] - pivot[m, j] * column[m]
                tile[u] = tile[u] - widen(column[m]) * rows[m]
        done.append(panel)
        if at + 1 + AHEAD < slabs:
            update = lax.dot_general(left_terms(panel[:, :LANES], 0), right_terms(panel), (((0,), (0,)), ((), ())),
                                     preferred_element_type=jnp.float32)
            for u in range(at + 1 + AHEAD, slabs):
                tile[u] = tile[u] - update[SUB * u:SUB * u + SUB]
    factored = jnp.concatenate(done, axis=0)
    return jnp.where(col >= row, factored[:, :LANES], 0.0), factored[:, LANES:]


def factor_kernel(even_ref, odd_ref, out_ref, gram_ref, factor_ref, column_ref, lead_ref, *, strips):
    total = gram_ref.shape[0]
    tiles = total // LANES
    height = LANES // strips
    mine = lax.axis_index("rows") & (strips - 1)
    block = 0
    for upper in range(tiles):
        for right in range(upper, tiles):
            for low_bit, in_ref in ((0, even_ref), (1, odd_ref)):
                for half in range(strips // 2):
                    strip = pl.multiple_of(((low_bit + 2 * half) ^ mine) * height, height)
                    gram_ref[pl.ds(upper * LANES + strip, height), right * LANES:(right + 1) * LANES] = in_ref[
                        half, block * height:(block + 1) * height, :]
            block += 1
    factor_ref[...] = jnp.zeros_like(factor_ref)
    for at in range(tiles):
        here = slice(at * LANES, (at + 1) * LANES)
        factor, inverse = factor_tile(gram_ref[here, here], column_ref, lead_ref)
        factor_ref[here, here] = factor
        if at < tiles - 1:
            rest = (at + 1) * LANES
            panel = times(inverse, gram_ref[here, rest:])
            factor_ref[here, rest:] = panel
            gram_ref[rest:, rest:] -= inner_product(panel, panel)
    width = out_ref.shape[1]
    first = pl.multiple_of(lax.axis_index("cols") * width, width)
    out_ref[...] = factor_ref[:, pl.ds(first, width)]


def factor_panel(even, odd, total, width):
    strips = 2 * even.shape[0]
    return pl.pallas_call(
        functools.partial(factor_kernel, strips=strips),
        out_shape=jax.ShapeDtypeStruct((total, width), jnp.float32),
        scratch_shapes=[pltpu.VMEM((total, total), jnp.float32)] * 2 + [
            pltpu.VMEM((LANES * SUB, LANES), jnp.float32), pltpu.VMEM((2 * LANES, LANES), jnp.float32)],
        compiler_params=pltpu.CompilerParams(vmem_limit_bytes=48 << 20),
    )(even, odd)


def reduce_run(keep, send, order):
    value = keep + swapped(send, "rows", 0)
    for bit in order:
        half = value.shape[0] // 2
        value = value[:half] + swapped(value[half:], "rows", bit)
    return value


def body(slab, sign_bits, block_mask, sample_rows):
    row_count, panel_width = slab.shape
    groups = lax.axis_size("rows")
    peers = lax.axis_size("cols")
    bits = groups.bit_length() - 1
    pick_count = sample_rows.shape[0]
    signs = sign_bits.reshape(row_count // LANES, LANES)
    picks = sample_rows
    runs = 4
    rows = row_count // runs
    mixed = []
    source = slab
    for bit in range(bits):
        other = swapped(picks, "rows", bit)
        run = bit - (bits - runs)
        if run >= 0:
            made = mix_run(source, signs, block_mask, run * rows, rows, mixed if run == runs - 1 else [])
            other, made, source = lax.optimization_barrier((other, made, source))
            mixed.append(made)
        picks = jnp.concatenate([picks, other])
    mixed = mixed[-1]
    first = pick_count // 2
    cross = list(range(1, bits))
    sketch = []
    pieces = []
    for start, count, order in ((0, first, cross), (first, pick_count - first, cross[1:2] + cross[:1] + cross[2:])):
        keep, send = pick_rows(picks, mixed, start, count, order, groups)
        part = reduce_run(keep, send, order)
        sketch.append(part)
        pieces.append(part)
        for peer in range(1, peers):
            pieces.append(lax.ppermute(part, "cols", [(i, i ^ peer) for i in range(peers)]))
    sketch = jnp.concatenate(sketch)
    keep, send = partial_gram(pieces, pick_count, peers, 4, 1.0 / (pick_count * groups))
    gram = keep + swapped(send, "rows", 0)
    gram = gram[:1] + swapped(gram[1:], "rows", 1)
    for bit in range(2, bits):
        gram = gram + swapped(gram, "rows", bit)
    gram = jnp.concatenate([gram, swapped(gram, "rows", 1)])
    r_panel = factor_panel(gram, swapped(gram, "rows", 0), panel_width * peers, panel_width)
    return (sketch, r_panel)


def solution(mesh):
    in_specs = (P("rows", "cols"), P("rows"), P("rows"), P("rows"))
    out_specs = (P("rows", "cols"), P(None, "cols"))
    return jax.shard_map(body, mesh=mesh, in_specs=in_specs, out_specs=out_specs, check_vma=False)
```

```python
import functools
import math

import jax
import jax.numpy as jnp
from jax import lax
from jax.experimental import pallas as pl
from jax.experimental.pallas import tpu as pltpu
from jax.sharding import PartitionSpec as P

TILE = 256
LANES = 128
SUB = 8
STRIPS = 8
AHEAD = 3
MIX_LIMIT = 32


def swapped(value, axis, bit):
    return lax.ppermute(value, axis, [(i, i ^ 1 << bit) for i in range(lax.axis_size(axis))])


def parity_sign(common):
    for shift in (16, 8, 4, 2, 1):
        common = common ^ (common >> shift)
    return 1 - 2 * (common & 1)


def butterfly(parts):
    stride = 1
    while stride < len(parts):
        for at in range(len(parts)):
            if at & stride == 0:
                low, high = parts[at], parts[at + stride]
                parts[at], parts[at + stride] = low + high, low - high
        stride *= 2
    return parts


def split_two(value):
    high = value.astype(jnp.bfloat16)
    low = (value - high.astype(jnp.float32)).astype(jnp.bfloat16)
    return high, low


def mix_kernel(mask_ref, slab_ref, sign_ref, *refs, first, earlier):
    joined = refs[:earlier]
    out_ref, had_ref = refs[earlier:]
    step = joined[0].shape[0] if earlier else out_ref.shape[0]
    base_out = earlier * step
    rows = out_ref.shape[0] - base_out
    row = lax.broadcasted_iota(jnp.int32, (TILE, TILE), 0)
    col = lax.broadcasted_iota(jnp.int32, (TILE, TILE), 1)
    had_ref[...] = parity_sign(row & col).astype(jnp.float32).astype(jnp.bfloat16)
    per_tile = TILE // LANES
    pair = 2
    for start in range(0, rows // TILE, pair):
        mixed = []
        for block in range(start, start + pair):
            signed = []
            for half in range(per_tile):
                at = first // LANES + block * per_tile + half
                sign = (2 * sign_ref[at:at + 1, :] - 1) * mask_ref[at]
                sign = sign.astype(jnp.float32).astype(jnp.bfloat16)
                signed.append(had_ref[:, half * LANES:(half + 1) * LANES] * sign)
            left = jnp.concatenate(signed * 2, axis=1)
            part = slab_ref[first + block * TILE:first + (block + 1) * TILE, :]
            right = jnp.concatenate(split_two(part), axis=0)
            mixed.append(jnp.dot(left, right, preferred_element_type=jnp.float32))
        mixed = butterfly(mixed)
        for block in range(pair):
            at = base_out + (start + block) * TILE
            out_ref[at:at + TILE, :] = mixed[block]

    span = pair * TILE
    for part in range(rows // step):
        @pl.loop(0, span // SUB // 4)
        def _(batch):
            for eighth in range(4):
                base = base_out + part * step + pl.multiple_of(batch * 4 * SUB, 4 * SUB) + eighth * SUB
                values = butterfly([out_ref[pl.ds(base + at * span, SUB), :] for at in range(step // span)])
                for at in range(step // span):
                    out_ref[pl.ds(base + at * span, SUB), :] = values[at]

    if earlier:
        @pl.loop(0, step // SUB // 8)
        def _(batch):
            for eighth in range(8):
                base = pl.multiple_of(batch * 8 * SUB, 8 * SUB) + eighth * SUB
                values = [ref[pl.ds(base, SUB), :] for ref in joined]
                for part in range(rows // step):
                    values.append(out_ref[pl.ds(base_out + part * step + base, SUB), :])
                values = butterfly(values)
                for at, value in enumerate(values):
                    out_ref[pl.ds(base + at * step, SUB), :] = value


def mix_run(slab, sign_bits, block_mask, first, rows, earlier):
    held = rows + sum(value.shape[0] for value in earlier)
    return pl.pallas_call(
        functools.partial(mix_kernel, first=first, earlier=len(earlier)),
        in_specs=[pl.BlockSpec(memory_space=pltpu.SMEM)] + [pl.BlockSpec(memory_space=pltpu.VMEM)] * (2 + len(earlier)),
        out_specs=pl.BlockSpec(memory_space=pltpu.VMEM),
        out_shape=jax.ShapeDtypeStruct((held, slab.shape[1]), jnp.float32),
        scratch_shapes=[pltpu.VMEM((TILE, TILE), jnp.bfloat16)],
        compiler_params=pltpu.CompilerParams(vmem_limit_bytes=MIX_LIMIT << 20),
    )(block_mask, slab, sign_bits, *earlier)


def pick_kernel(pick_ref, mixed_ref, keep_ref, send_ref, *, start, count, order, pick_count, groups, norm_scale):
    device = lax.axis_index("rows")
    sub_row = lax.broadcasted_iota(jnp.int32, (SUB, mixed_ref.shape[1]), 0)
    octets = count // SUB
    for out_ref, low_bit in ((send_ref, 1), (keep_ref, 0)):
        @pl.loop(0, groups // 2)
        def _(pair):
            offset = low_bit
            for place, bit in enumerate(reversed(order)):
                offset = offset | ((pair >> place) & 1) << bit
            scale = parity_sign((device ^ offset) & device).astype(jnp.float32) * norm_scale
            for octet in range(octets):
                rows = None
                for sub in range(SUB):
                    index = pick_ref[offset * pick_count + start + octet * SUB + sub]
                    taken = jnp.broadcast_to(mixed_ref[pl.ds(index, 1), :], sub_row.shape)
                    rows = taken if rows is None else jnp.where(sub_row == sub, taken, rows)
                out_at = pl.multiple_of(pair * count + octet * SUB, SUB)
                out_ref[pl.ds(out_at, SUB), :] = rows * scale


def pick_rows(picks, mixed, start, count, order, groups):
    norm_scale = 1.0 / math.sqrt(mixed.shape[0] * groups)
    half = jax.ShapeDtypeStruct((groups // 2 * count, mixed.shape[1]), jnp.float32)
    return pl.pallas_call(
        functools.partial(pick_kernel, start=start, count=count, order=order, pick_count=picks.shape[0] // groups,
                          groups=groups, norm_scale=norm_scale),
        in_specs=[pl.BlockSpec(memory_space=pltpu.SMEM), pl.BlockSpec(memory_space=pltpu.VMEM)],
        out_specs=[pl.BlockSpec(memory_space=pltpu.VMEM)] * 2,
        out_shape=[half, half],
        compiler_params=pltpu.CompilerParams(vmem_limit_bytes=32 << 20),
    )(picks, mixed)


def strip_bits(group):
    return (0, 1, 2) if group == 0 else (0, 2, 1)


def block_groups(tiles):
    pairs = [(i, j) for i in range(tiles) for j in range(i, tiles)]
    return [pairs[:len(pairs) // 2], pairs[len(pairs) // 2:]]


def strip_starts(group, low_bit):
    height = LANES // STRIPS
    mine = lax.axis_index("rows") & (STRIPS - 1)
    order = strip_bits(group)
    starts = []
    for slot in range(STRIPS // 2):
        offset = low_bit | (slot >> 1) << order[1] | (slot & 1) << order[2]
        starts.append(pl.multiple_of((mine ^ offset) * height, height))
    return starts


def gram_kernel(*refs, scale, peers, groups):
    outs = 2 * len(groups)
    pieces, out_refs, (full_ref, gram_ref) = refs[:-outs - 2], refs[-outs - 2:-2], refs[-2:]
    total = full_ref.shape[1]
    width = total // peers
    column = lax.axis_index("cols")
    at = 0
    for run in range(len(pieces) // peers):
        count = pieces[run * peers].shape[0]
        for peer in range(peers):
            first = pl.multiple_of((column ^ peer) * width, width)
            full_ref[at:at + count, pl.ds(first, width)] = pieces[run * peers + peer][...]
        at += count
    for upper in range(total // LANES):
        here = slice(upper * LANES, (upper + 1) * LANES)
        rows = lax.dot_general(full_ref[:, here], full_ref[:, upper * LANES:], (((0,), (0,)), ((), ())),
                               precision=lax.Precision.HIGHEST, preferred_element_type=jnp.float32)
        gram_ref[here, upper * LANES:] = rows * scale
    height = LANES // STRIPS
    for group, pairs in enumerate(groups):
        for low_bit in range(2):
            for slot, strip in enumerate(strip_starts(group, low_bit)):
                for block, (upper, right) in enumerate(pairs):
                    out_refs[2 * group + low_bit][slot, block * height:(block + 1) * height, :] = gram_ref[
                        pl.ds(upper * LANES + strip, height), right * LANES:(right + 1) * LANES]


def partial_gram(pieces, rows, peers, scale):
    total = pieces[0].shape[1] * peers
    groups = block_groups(total // LANES)
    shapes = []
    for pairs in groups:
        shapes += [jax.ShapeDtypeStruct((STRIPS // 2, len(pairs) * (LANES // STRIPS), LANES), jnp.float32)] * 2
    return pl.pallas_call(
        functools.partial(gram_kernel, scale=scale, peers=peers, groups=groups),
        out_shape=shapes,
        scratch_shapes=[pltpu.VMEM((rows, total), jnp.float32), pltpu.VMEM((total, total), jnp.float32)],
        compiler_params=pltpu.CompilerParams(vmem_limit_bytes=16 << 20),
    )(*pieces)


def split_three(value):
    high = value.astype(jnp.bfloat16).astype(jnp.float32)
    rest = value - high
    middle = rest.astype(jnp.bfloat16).astype(jnp.float32)
    return high, middle, rest - middle


def left_terms(value, axis):
    high, middle, low = split_three(value)
    return jnp.concatenate([high, high, middle, high, middle, low], axis=axis).astype(jnp.bfloat16)


def right_terms(value):
    high, middle, low = split_three(value)
    return jnp.concatenate([high, middle, high, low, middle, high], axis=0).astype(jnp.bfloat16)


def times(left, right):
    return jnp.dot(left_terms(left, 1), right_terms(right), preferred_element_type=jnp.float32)


def inner_product(left, right):
    return lax.dot_general(left_terms(left, 0), right_terms(right), (((0,), (0,)), ((), ())),
                           preferred_element_type=jnp.float32)


def lane_splat(value, lane):
    return jnp.broadcast_to(value[:, lane:lane + 1], (value.shape[0], LANES))


def factor_tile(diagonal, column_ref, lead_ref):
    row = lax.broadcasted_iota(jnp.int32, (LANES, LANES), 0)
    col = lax.broadcasted_iota(jnp.int32, (LANES, LANES), 1)
    identity = (row == col).astype(jnp.float32)
    whole = jnp.concatenate([diagonal, identity], axis=1)
    slabs = LANES // SUB
    tile = [whole[SUB * t:SUB * t + SUB] for t in range(slabs)]
    sub_row = lax.broadcasted_iota(jnp.int32, tile[0].shape, 0)
    done = []

    def widen(value):
        return jnp.concatenate([value, value], axis=1)

    for at in range(slabs):
        lead = tile[at]
        direct = range(at + 1, min(slabs, at + 1 + AHEAD))
        for j in range(SUB):
            column_ref[(at * SUB + j) * SUB:(at * SUB + j + 1) * SUB, :] = lane_splat(lead[:, :LANES], SUB * at + j)
        for half in range(2):
            lead_ref[half * LANES + at * SUB:half * LANES + (at + 1) * SUB, :] = lead[:, half * LANES:(half + 1) * LANES]
        pivot = {(i, j): column_ref[pl.ds((at * SUB + j) * SUB + i, SUB, stride=0), :]
                 for j in range(SUB) for i in range(j + 1)}
        below = [[lane_splat(tile[u][:, :LANES], SUB * at + j) for j in range(SUB)] for u in direct]
        rows = [jnp.concatenate([lead_ref[pl.ds(half * LANES + at * SUB + m, SUB, stride=0), :] for half in range(2)],
                                axis=1) for m in range(SUB)]
        panel = jnp.zeros_like(lead)
        for m in range(SUB):
            inverse = lax.rsqrt(pivot[m, m])
            for j in range(m + 1, SUB):
                pivot[m, j] = pivot[m, j] * inverse
            for i in range(m + 1, SUB):
                for j in range(i, SUB):
                    pivot[i, j] = pivot[i, j] - pivot[m, i] * pivot[m, j]
            rows[m] = rows[m] * widen(inverse)
            for j in range(m + 1, SUB):
                rows[j] = rows[j] - widen(pivot[m, j]) * rows[m]
            panel = jnp.where(sub_row == m, rows[m], panel)
            for column, u in zip(below, direct):
                column[m] = column[m] * inverse
                for j in range(m + 1, SUB):
                    column[j] = column[j] - pivot[m, j] * column[m]
                tile[u] = tile[u] - widen(column[m]) * rows[m]
        done.append(panel)
        if at + 1 + AHEAD < slabs:
            update = lax.dot_general(left_terms(panel[:, :LANES], 0), right_terms(panel), (((0,), (0,)), ((), ())),
                                     preferred_element_type=jnp.float32)
            for u in range(at + 1 + AHEAD, slabs):
                tile[u] = tile[u] - update[SUB * u:SUB * u + SUB]
    factored = jnp.concatenate(done, axis=0)
    return jnp.where(col >= row, factored[:, :LANES], 0.0), factored[:, LANES:]


def factor_kernel(*refs, groups):
    strip_refs, (out_ref, gram_ref, factor_ref, column_ref, lead_ref) = refs[:-5], refs[-5:]
    tiles = gram_ref.shape[0] // LANES
    height = LANES // STRIPS
    for group, pairs in enumerate(groups):
        for low_bit in range(2):
            for slot, strip in enumerate(strip_starts(group, low_bit)):
                for block, (upper, right) in enumerate(pairs):
                    gram_ref[pl.ds(upper * LANES + strip, height), right * LANES:(right + 1) * LANES] = strip_refs[
                        2 * group + low_bit][slot, block * height:(block + 1) * height, :]
    factor_ref[...] = jnp.zeros_like(factor_ref)
    for at in range(tiles):
        here = slice(at * LANES, (at + 1) * LANES)
        factor, inverse = factor_tile(gram_ref[here, here], column_ref, lead_ref)
        factor_ref[here, here] = factor
        if at < tiles - 1:
            rest = (at + 1) * LANES
            panel = times(inverse, gram_ref[here, rest:])
            factor_ref[here, rest:] = panel
            gram_ref[rest:, rest:] -= inner_product(panel, panel)
    width = out_ref.shape[1]
    first = pl.multiple_of(lax.axis_index("cols") * width, width)
    out_ref[...] = factor_ref[:, pl.ds(first, width)]


def factor_panel(strips, total, width):
    return pl.pallas_call(
        functools.partial(factor_kernel, groups=block_groups(total // LANES)),
        out_shape=jax.ShapeDtypeStruct((total, width), jnp.float32),
        scratch_shapes=[pltpu.VMEM((total, total), jnp.float32)] * 2 + [
            pltpu.VMEM((LANES * SUB, LANES), jnp.float32), pltpu.VMEM((2 * LANES, LANES), jnp.float32)],
        compiler_params=pltpu.CompilerParams(vmem_limit_bytes=16 << 20),
    )(*strips)


def summed_strips(keep, send, group, bits):
    core, *order = strip_bits(group)
    gram = keep + swapped(send, "rows", core)
    for bit in order:
        half = gram.shape[0] // 2
        gram = gram[:half] + swapped(gram[half:], "rows", bit)
    for bit in range(len(order) + 1, bits):
        gram = gram + swapped(gram, "rows", bit)
    for bit in reversed(order):
        gram = jnp.concatenate([gram, swapped(gram, "rows", bit)])
    return [gram, swapped(gram, "rows", core)]


def reduce_run(keep, send, order):
    value = keep + swapped(send, "rows", 0)
    for bit in order:
        half = value.shape[0] // 2
        value = value[:half] + swapped(value[half:], "rows", bit)
    return value


def body(slab, sign_bits, block_mask, sample_rows):
    row_count, panel_width = slab.shape
    groups = lax.axis_size("rows")
    peers = lax.axis_size("cols")
    bits = groups.bit_length() - 1
    pick_count = sample_rows.shape[0]
    signs = sign_bits.reshape(row_count // LANES, LANES)
    picks = sample_rows
    step = row_count // 4
    mixed = []
    source = slab
    for bit in range(bits):
        run = bit - (bits - 3)
        if run == 0:
            picks, signs = lax.optimization_barrier((picks, signs))
        other = swapped(picks, "rows", bit)
        if run >= 0:
            last = run == 2
            made = mix_run(source, signs, block_mask, run * step, 2 * step if last else step, mixed if last else [])
            other, made, source = lax.optimization_barrier((other, made, source))
            mixed.append(made)
        picks = jnp.concatenate([picks, other])
    mixed = mixed[-1]
    first = pick_count // 2
    cross = list(range(1, bits))
    sketch = []
    pieces = []
    for start, count, order in ((0, first, cross), (first, pick_count - first, cross[1:2] + cross[:1] + cross[2:])):
        keep, send = pick_rows(picks, mixed, start, count, order, groups)
        part = reduce_run(keep, send, order)
        sketch.append(part)
        pieces.append(part)
        for peer in range(1, peers):
            pieces.append(lax.ppermute(part, "cols", [(i, i ^ peer) for i in range(peers)]))
    sketch = jnp.concatenate(sketch)
    parts = partial_gram(pieces, pick_count, peers, 1.0 / (pick_count * groups))
    strips = []
    for group in range(len(parts) // 2):
        strips += summed_strips(parts[2 * group], parts[2 * group + 1], group, bits)
    r_panel = factor_panel(strips, panel_width * peers, panel_width)
    return (sketch, r_panel)


def solution(mesh):
    in_specs = (P("rows", "cols"), P("rows"), P("rows"), P("rows"))
    out_specs = (P("rows", "cols"), P(None, "cols"))
    return jax.shard_map(body, mesh=mesh, in_specs=in_specs, out_specs=out_specs, check_vma=False)
```

```python
import functools
import math

import jax
import jax.numpy as jnp
from jax import lax
from jax.experimental import pallas as pl
from jax.experimental.pallas import tpu as pltpu
from jax.sharding import PartitionSpec as P

TILE = 256
LANES = 128
SUB = 8
STRIPS = 8
AHEAD = 3
FIRST_LIMIT = 40


def swapped(value, axis, bit):
    return lax.ppermute(value, axis, [(i, i ^ 1 << bit) for i in range(lax.axis_size(axis))])


def parity_sign(common):
    for shift in (16, 8, 4, 2, 1):
        common = common ^ (common >> shift)
    return 1 - 2 * (common & 1)


def butterfly(parts):
    stride = 1
    while stride < len(parts):
        for at in range(len(parts)):
            if at & stride == 0:
                low, high = parts[at], parts[at + stride]
                parts[at], parts[at + stride] = low + high, low - high
        stride *= 2
    return parts


def split_two(value):
    high = value.astype(jnp.bfloat16)
    low = (value - high.astype(jnp.float32)).astype(jnp.bfloat16)
    return high, low


def fill_hadamard(had_ref):
    row = lax.broadcasted_iota(jnp.int32, (TILE, TILE), 0)
    col = lax.broadcasted_iota(jnp.int32, (TILE, TILE), 1)
    had_ref[...] = parity_sign(row & col).astype(jnp.float32).astype(jnp.bfloat16)


def mix_tiles(source_ref, sign_ref, had_ref, out_ref, source_at, sign_at, out_at, count):
    per_tile = TILE // LANES
    mixed = []
    for block in range(count):
        signed = []
        for half in range(per_tile):
            at = sign_at // LANES + block * per_tile + half
            sign = sign_ref[at:at + 1, :].astype(jnp.bfloat16)
            signed.append(had_ref[:, half * LANES:(half + 1) * LANES] * sign)
        left = jnp.concatenate(signed * 2, axis=1)
        part = source_ref[source_at + block * TILE:source_at + (block + 1) * TILE, :]
        right = jnp.concatenate(split_two(part), axis=0)
        mixed.append(jnp.dot(left, right, preferred_element_type=jnp.float32))
    mixed = butterfly(mixed)
    for block in range(count):
        at = out_at + block * TILE
        out_ref[at:at + TILE, :] = mixed[block]


def join_runs(refs, starts, out_ref, out_starts, rows, unroll):
    @pl.loop(0, rows // (SUB * unroll))
    def _(batch):
        for sub in range(unroll):
            base = pl.multiple_of(batch * SUB * unroll, SUB * unroll) + sub * SUB
            values = butterfly([ref[pl.ds(start + base, SUB), :] for ref, start in zip(refs, starts)])
            for start, value in zip(out_starts, values):
                out_ref[pl.ds(start + base, SUB), :] = value


def mix_first_kernel(slab_ref, sign_ref, out_ref, rest_ref, had_ref, buf_ref, sems, *, quarter):
    pair = 2
    span = pair * TILE
    chunks = quarter // span

    def fetch(part):
        rows = pl.ds(part * span, span)
        if part < 2 * chunks:
            target = buf_ref.at[rows, :]
        else:
            target = rest_ref.at[pl.ds((part - 2 * chunks) * span, span), :]
        return pltpu.make_async_copy(slab_ref.at[rows, :], target, sems.at[part])

    for part in range(4 * chunks):
        fetch(part).start()
    fill_hadamard(had_ref)
    for half in range(2):
        for part in range(half * chunks, (half + 1) * chunks):
            fetch(part).wait()
            mix_tiles(buf_ref, sign_ref, had_ref, out_ref, part * span, part * span, part * span, pair)
        starts = [half * quarter + at * span for at in range(chunks)]
        join_runs([out_ref] * chunks, starts, out_ref, starts, span, 4)
    for part in range(2 * chunks, 4 * chunks):
        fetch(part).wait()


def mix_next_kernel(rest_ref, sign_ref, *refs, at, earlier, quarter):
    joined = refs[:earlier]
    out_ref, had_ref = refs[earlier:]
    pair = 2
    span = pair * TILE
    chunks = quarter // span
    base = out_ref.shape[0] - quarter
    fill_hadamard(had_ref)
    for part in range(chunks):
        mix_tiles(rest_ref, sign_ref, had_ref, out_ref, (at - 2) * quarter + part * span,
                  at * quarter + part * span, base + part * span, pair)
    starts = [base + part * span for part in range(chunks)]
    join_runs([out_ref] * chunks, starts, out_ref, starts, span, 4)
    if earlier:
        sources, starts = [], []
        for ref in joined:
            for start in range(0, ref.shape[0], quarter):
                sources.append(ref)
                starts.append(start)
        join_runs(sources + [out_ref], starts + [base], out_ref, range(0, 4 * quarter, quarter), quarter, 8)


def mix_first(slab, signs):
    rows, width = slab.shape
    half = jax.ShapeDtypeStruct((rows // 2, width), jnp.float32)
    return pl.pallas_call(
        functools.partial(mix_first_kernel, quarter=rows // 4),
        in_specs=[pl.BlockSpec(memory_space=pltpu.HBM), pl.BlockSpec(memory_space=pltpu.VMEM)],
        out_specs=[pl.BlockSpec(memory_space=pltpu.VMEM)] * 2,
        out_shape=[half, half],
        scratch_shapes=[
            pltpu.VMEM((TILE, TILE), jnp.bfloat16),
            pltpu.VMEM(half.shape, jnp.float32),
            pltpu.SemaphoreType.DMA((rows // (2 * TILE),)),
        ],
        compiler_params=pltpu.CompilerParams(vmem_limit_bytes=FIRST_LIMIT << 20),
    )(slab, signs)


def mix_next(rest, signs, at, earlier):
    quarter = rest.shape[0] // 2
    held = quarter + sum(value.shape[0] for value in earlier)
    return pl.pallas_call(
        functools.partial(mix_next_kernel, at=at, earlier=len(earlier), quarter=quarter),
        in_specs=[pl.BlockSpec(memory_space=pltpu.VMEM)] * (2 + len(earlier)),
        out_specs=pl.BlockSpec(memory_space=pltpu.VMEM),
        out_shape=jax.ShapeDtypeStruct((held, rest.shape[1]), jnp.float32),
        scratch_shapes=[pltpu.VMEM((TILE, TILE), jnp.bfloat16)],
        compiler_params=pltpu.CompilerParams(vmem_limit_bytes=32 << 20),
    )(rest, signs, *earlier)


def pick_kernel(pick_ref, mixed_ref, keep_ref, send_ref, *, start, count, order, pick_count, groups, norm_scale):
    device = lax.axis_index("rows")
    sub_row = lax.broadcasted_iota(jnp.int32, (SUB, mixed_ref.shape[1]), 0)
    octets = count // SUB
    for out_ref, low_bit in ((send_ref, 1), (keep_ref, 0)):
        @pl.loop(0, groups // 2)
        def _(pair):
            offset = low_bit
            for place, bit in enumerate(reversed(order)):
                offset = offset | ((pair >> place) & 1) << bit
            scale = parity_sign((device ^ offset) & device).astype(jnp.float32) * norm_scale
            for octet in range(octets):
                rows = None
                for sub in range(SUB):
                    index = pick_ref[offset * pick_count + start + octet * SUB + sub]
                    taken = jnp.broadcast_to(mixed_ref[pl.ds(index, 1), :], sub_row.shape)
                    rows = taken if rows is None else jnp.where(sub_row == sub, taken, rows)
                out_at = pl.multiple_of(pair * count + octet * SUB, SUB)
                out_ref[pl.ds(out_at, SUB), :] = rows * scale


def pick_rows(picks, mixed, start, count, order, groups):
    norm_scale = 1.0 / math.sqrt(mixed.shape[0] * groups)
    half = jax.ShapeDtypeStruct((groups // 2 * count, mixed.shape[1]), jnp.float32)
    return pl.pallas_call(
        functools.partial(pick_kernel, start=start, count=count, order=order, pick_count=picks.shape[0] // groups,
                          groups=groups, norm_scale=norm_scale),
        in_specs=[pl.BlockSpec(memory_space=pltpu.SMEM), pl.BlockSpec(memory_space=pltpu.VMEM)],
        out_specs=[pl.BlockSpec(memory_space=pltpu.VMEM)] * 2,
        out_shape=[half, half],
        compiler_params=pltpu.CompilerParams(vmem_limit_bytes=32 << 20),
    )(picks, mixed)


def strip_bits(group):
    return (0, 1, 2) if group == 0 else (0, 2, 1)


def block_groups(tiles):
    pairs = [(i, j) for i in range(tiles) for j in range(i, tiles)]
    return [pairs[:len(pairs) // 2], pairs[len(pairs) // 2:]]


def strip_starts(group, low_bit):
    height = LANES // STRIPS
    mine = lax.axis_index("rows") & (STRIPS - 1)
    order = strip_bits(group)
    starts = []
    for slot in range(STRIPS // 2):
        offset = low_bit | (slot >> 1) << order[1] | (slot & 1) << order[2]
        starts.append(pl.multiple_of((mine ^ offset) * height, height))
    return starts


def gram_kernel(*refs, scale, peers, groups):
    outs = 2 * len(groups)
    pieces, out_refs, (full_ref, gram_ref) = refs[:-outs - 2], refs[-outs - 2:-2], refs[-2:]
    total = full_ref.shape[1]
    width = total // peers
    column = lax.axis_index("cols")
    at = 0
    for run in range(len(pieces) // peers):
        count = pieces[run * peers].shape[0]
        for peer in range(peers):
            first = pl.multiple_of((column ^ peer) * width, width)
            full_ref[at:at + count, pl.ds(first, width)] = pieces[run * peers + peer][...]
        at += count
    for upper in range(total // LANES):
        here = slice(upper * LANES, (upper + 1) * LANES)
        rows = lax.dot_general(full_ref[:, here], full_ref[:, upper * LANES:], (((0,), (0,)), ((), ())),
                               precision=lax.Precision.HIGHEST, preferred_element_type=jnp.float32)
        gram_ref[here, upper * LANES:] = rows * scale
    height = LANES // STRIPS
    for group, pairs in enumerate(groups):
        for low_bit in range(2):
            for slot, strip in enumerate(strip_starts(group, low_bit)):
                for block, (upper, right) in enumerate(pairs):
                    out_refs[2 * group + low_bit][slot, block * height:(block + 1) * height, :] = gram_ref[
                        pl.ds(upper * LANES + strip, height), right * LANES:(right + 1) * LANES]


def partial_gram(pieces, rows, peers, scale):
    total = pieces[0].shape[1] * peers
    groups = block_groups(total // LANES)
    shapes = []
    for pairs in groups:
        shapes += [jax.ShapeDtypeStruct((STRIPS // 2, len(pairs) * (LANES // STRIPS), LANES), jnp.float32)] * 2
    return pl.pallas_call(
        functools.partial(gram_kernel, scale=scale, peers=peers, groups=groups),
        out_shape=shapes,
        scratch_shapes=[pltpu.VMEM((rows, total), jnp.float32), pltpu.VMEM((total, total), jnp.float32)],
        compiler_params=pltpu.CompilerParams(vmem_limit_bytes=16 << 20),
    )(*pieces)


def split_three(value):
    high = value.astype(jnp.bfloat16).astype(jnp.float32)
    rest = value - high
    middle = rest.astype(jnp.bfloat16).astype(jnp.float32)
    return high, middle, rest - middle


def left_terms(value, axis):
    high, middle, low = split_three(value)
    return jnp.concatenate([high, high, middle, high, middle, low], axis=axis).astype(jnp.bfloat16)


def right_terms(value):
    high, middle, low = split_three(value)
    return jnp.concatenate([high, middle, high, low, middle, high], axis=0).astype(jnp.bfloat16)


def times(left, right):
    return jnp.dot(left_terms(left, 1), right_terms(right), preferred_element_type=jnp.float32)


def inner_product(left, right):
    return lax.dot_general(left_terms(left, 0), right_terms(right), (((0,), (0,)), ((), ())),
                           preferred_element_type=jnp.float32)


def lane_splat(value, lane):
    return jnp.broadcast_to(value[:, lane:lane + 1], (value.shape[0], LANES))


def factor_tile(diagonal, column_ref, lead_ref):
    row = lax.broadcasted_iota(jnp.int32, (LANES, LANES), 0)
    col = lax.broadcasted_iota(jnp.int32, (LANES, LANES), 1)
    identity = (row == col).astype(jnp.float32)
    whole = jnp.concatenate([diagonal, identity], axis=1)
    slabs = LANES // SUB
    tile = [whole[SUB * t:SUB * t + SUB] for t in range(slabs)]
    sub_row = lax.broadcasted_iota(jnp.int32, tile[0].shape, 0)
    done = []

    def widen(value):
        return jnp.concatenate([value, value], axis=1)

    for at in range(slabs):
        lead = tile[at]
        direct = range(at + 1, min(slabs, at + 1 + AHEAD))
        for j in range(SUB):
            column_ref[(at * SUB + j) * SUB:(at * SUB + j + 1) * SUB, :] = lane_splat(lead[:, :LANES], SUB * at + j)
        for half in range(2):
            lead_ref[half * LANES + at * SUB:half * LANES + (at + 1) * SUB, :] = lead[:, half * LANES:(half + 1) * LANES]
        pivot = {(i, j): column_ref[pl.ds((at * SUB + j) * SUB + i, SUB, stride=0), :]
                 for j in range(SUB) for i in range(j + 1)}
        below = [[lane_splat(tile[u][:, :LANES], SUB * at + j) for j in range(SUB)] for u in direct]
        rows = [jnp.concatenate([lead_ref[pl.ds(half * LANES + at * SUB + m, SUB, stride=0), :] for half in range(2)],
                                axis=1) for m in range(SUB)]
        panel = jnp.zeros_like(lead)
        for m in range(SUB):
            inverse = lax.rsqrt(pivot[m, m])
            for j in range(m + 1, SUB):
                pivot[m, j] = pivot[m, j] * inverse
            for i in range(m + 1, SUB):
                for j in range(i, SUB):
                    pivot[i, j] = pivot[i, j] - pivot[m, i] * pivot[m, j]
            rows[m] = rows[m] * widen(inverse)
            for j in range(m + 1, SUB):
                rows[j] = rows[j] - widen(pivot[m, j]) * rows[m]
            panel = jnp.where(sub_row == m, rows[m], panel)
            for column, u in zip(below, direct):
                column[m] = column[m] * inverse
                for j in range(m + 1, SUB):
                    column[j] = column[j] - pivot[m, j] * column[m]
                tile[u] = tile[u] - widen(column[m]) * rows[m]
        done.append(panel)
        if at + 1 + AHEAD < slabs:
            update = lax.dot_general(left_terms(panel[:, :LANES], 0), right_terms(panel), (((0,), (0,)), ((), ())),
                                     preferred_element_type=jnp.float32)
            for u in range(at + 1 + AHEAD, slabs):
                tile[u] = tile[u] - update[SUB * u:SUB * u + SUB]
    factored = jnp.concatenate(done, axis=0)
    return jnp.where(col >= row, factored[:, :LANES], 0.0), factored[:, LANES:]


def factor_kernel(*refs, groups):
    strip_refs, (out_ref, gram_ref, factor_ref, column_ref, lead_ref) = refs[:-5], refs[-5:]
    tiles = gram_ref.shape[0] // LANES
    height = LANES // STRIPS
    for group, pairs in enumerate(groups):
        for low_bit in range(2):
            for slot, strip in enumerate(strip_starts(group, low_bit)):
                for block, (upper, right) in enumerate(pairs):
                    gram_ref[pl.ds(upper * LANES + strip, height), right * LANES:(right + 1) * LANES] = strip_refs[
                        2 * group + low_bit][slot, block * height:(block + 1) * height, :]
    factor_ref[...] = jnp.zeros_like(factor_ref)
    for at in range(tiles):
        here = slice(at * LANES, (at + 1) * LANES)
        factor, inverse = factor_tile(gram_ref[here, here], column_ref, lead_ref)
        factor_ref[here, here] = factor
        if at < tiles - 1:
            rest = (at + 1) * LANES
            panel = times(inverse, gram_ref[here, rest:])
            factor_ref[here, rest:] = panel
            gram_ref[rest:, rest:] -= inner_product(panel, panel)
    width = out_ref.shape[1]
    first = pl.multiple_of(lax.axis_index("cols") * width, width)
    out_ref[...] = factor_ref[:, pl.ds(first, width)]


def factor_panel(strips, total, width):
    return pl.pallas_call(
        functools.partial(factor_kernel, groups=block_groups(total // LANES)),
        out_shape=jax.ShapeDtypeStruct((total, width), jnp.float32),
        scratch_shapes=[pltpu.VMEM((total, total), jnp.float32)] * 2 + [
            pltpu.VMEM((LANES * SUB, LANES), jnp.float32), pltpu.VMEM((2 * LANES, LANES), jnp.float32)],
        compiler_params=pltpu.CompilerParams(vmem_limit_bytes=16 << 20),
    )(*strips)


def summed_strips(keep, send, group, bits):
    core, *order = strip_bits(group)
    gram = keep + swapped(send, "rows", core)
    for bit in order:
        half = gram.shape[0] // 2
        gram = gram[:half] + swapped(gram[half:], "rows", bit)
    for bit in range(len(order) + 1, bits):
        gram = gram + swapped(gram, "rows", bit)
    for bit in reversed(order):
        gram = jnp.concatenate([gram, swapped(gram, "rows", bit)])
    return [gram, swapped(gram, "rows", core)]


def reduce_run(keep, send, order):
    value = keep + swapped(send, "rows", 0)
    for bit in order:
        half = value.shape[0] // 2
        value = value[:half] + swapped(value[half:], "rows", bit)
    return value


def body(slab, sign_bits, block_mask, sample_rows):
    row_count, panel_width = slab.shape
    groups = lax.axis_size("rows")
    peers = lax.axis_size("cols")
    bits = groups.bit_length() - 1
    pick_count = sample_rows.shape[0]
    blocks = block_mask.shape[0]
    signs = (2 * sign_bits - 1).reshape(blocks, row_count // blocks) * block_mask.reshape(blocks, 1)
    signs = signs.reshape(row_count // LANES, LANES).astype(jnp.float32)
    picks = sample_rows
    mixed = []
    for bit in range(bits):
        run = bit - (bits - 3)
        if run == 0:
            picks, signs = lax.optimization_barrier((picks, signs))
        other = swapped(picks, "rows", bit)
        if run == 0:
            made, rest = mix_first(slab, signs)
        elif run > 0:
            made = mix_next(rest, signs, run + 1, mixed if run == 2 else [])
        if run >= 0:
            other, made, rest = lax.optimization_barrier((other, made, rest))
            mixed.append(made)
        picks = jnp.concatenate([picks, other])
    mixed = mixed[-1]
    first = pick_count // 2
    cross = list(range(1, bits))
    sketch = []
    pieces = []
    for start, count, order in ((0, first, cross), (first, pick_count - first, cross[1:2] + cross[:1] + cross[2:])):
        keep, send = pick_rows(picks, mixed, start, count, order, groups)
        part = reduce_run(keep, send, order)
        sketch.append(part)
        pieces.append(part)
        for peer in range(1, peers):
            pieces.append(lax.ppermute(part, "cols", [(i, i ^ peer) for i in range(peers)]))
    sketch = jnp.concatenate(sketch)
    parts = partial_gram(pieces, pick_count, peers, 1.0 / (pick_count * groups))
    strips = []
    for group in range(len(parts) // 2):
        strips += summed_strips(parts[2 * group], parts[2 * group + 1], group, bits)
    r_panel = factor_panel(strips, panel_width * peers, panel_width)
    return (sketch, r_panel)


def solution(mesh):
    in_specs = (P("rows", "cols"), P("rows"), P("rows"), P("rows"))
    out_specs = (P("rows", "cols"), P(None, "cols"))
    return jax.shard_map(body, mesh=mesh, in_specs=in_specs, out_specs=out_specs, check_vma=False)
```

```python
import functools
import math

import jax
import jax.numpy as jnp
from jax import lax
from jax.experimental import pallas as pl
from jax.experimental.pallas import tpu as pltpu
from jax.sharding import PartitionSpec as P

TILE = 256
LANES = 128
SUB = 8
STRIPS = 8
AHEAD = 3
FIRST_LIMIT = 40


def swapped(value, axis, bit):
    return lax.ppermute(value, axis, [(i, i ^ 1 << bit) for i in range(lax.axis_size(axis))])


def parity_sign(common):
    for shift in (16, 8, 4, 2, 1):
        common = common ^ (common >> shift)
    return 1 - 2 * (common & 1)


def butterfly(parts):
    stride = 1
    while stride < len(parts):
        for at in range(len(parts)):
            if at & stride == 0:
                low, high = parts[at], parts[at + stride]
                parts[at], parts[at + stride] = low + high, low - high
        stride *= 2
    return parts


def split_two(value):
    high = value.astype(jnp.bfloat16)
    low = (value - high.astype(jnp.float32)).astype(jnp.bfloat16)
    return high, low


def fill_hadamard(had_ref):
    row = lax.broadcasted_iota(jnp.int32, (TILE, TILE), 0)
    col = lax.broadcasted_iota(jnp.int32, (TILE, TILE), 1)
    had_ref[...] = parity_sign(row & col).astype(jnp.float32).astype(jnp.bfloat16)


def mix_tiles(source_ref, sign_ref, had_ref, out_ref, source_at, sign_at, out_at, count):
    per_tile = TILE // LANES
    mixed = []
    for block in range(count):
        signed = []
        for half in range(per_tile):
            at = sign_at // LANES + block * per_tile + half
            sign = sign_ref[at:at + 1, :].astype(jnp.bfloat16)
            signed.append(had_ref[:, half * LANES:(half + 1) * LANES] * sign)
        left = jnp.concatenate(signed * 2, axis=1)
        part = source_ref[source_at + block * TILE:source_at + (block + 1) * TILE, :]
        right = jnp.concatenate(split_two(part), axis=0)
        mixed.append(jnp.dot(left, right, preferred_element_type=jnp.float32))
    mixed = butterfly(mixed)
    for block in range(count):
        at = out_at + block * TILE
        out_ref[at:at + TILE, :] = mixed[block]


def join_runs(refs, starts, out_ref, out_starts, rows, unroll):
    @pl.loop(0, rows // (SUB * unroll))
    def _(batch):
        for sub in range(unroll):
            base = pl.multiple_of(batch * SUB * unroll, SUB * unroll) + sub * SUB
            values = butterfly([ref[pl.ds(start + base, SUB), :] for ref, start in zip(refs, starts)])
            for start, value in zip(out_starts, values):
                out_ref[pl.ds(start + base, SUB), :] = value


def mix_first_kernel(slab_ref, sign_ref, out_ref, rest_ref, had_ref, buf_ref, sems, *, quarter):
    pair = 2
    span = pair * TILE
    chunks = quarter // span

    def fetch(part):
        rows = pl.ds(part * span, span)
        if part < 2 * chunks:
            target = buf_ref.at[rows, :]
        else:
            target = rest_ref.at[pl.ds((part - 2 * chunks) * span, span), :]
        return pltpu.make_async_copy(slab_ref.at[rows, :], target, sems.at[part])

    for part in range(4 * chunks):
        fetch(part).start()
    fill_hadamard(had_ref)
    for half in range(2):
        for part in range(half * chunks, (half + 1) * chunks):
            fetch(part).wait()
            mix_tiles(buf_ref, sign_ref, had_ref, out_ref, part * span, part * span, part * span, pair)
        starts = [half * quarter + at * span for at in range(chunks)]
        join_runs([out_ref] * chunks, starts, out_ref, starts, span, 4)
    for part in range(2 * chunks, 4 * chunks):
        fetch(part).wait()


def mix_next_kernel(rest_ref, sign_ref, out_ref, had_ref, *, quarter):
    pair = 2
    span = pair * TILE
    chunks = quarter // span
    fill_hadamard(had_ref)
    for half in range(2):
        for part in range(half * chunks, (half + 1) * chunks):
            mix_tiles(rest_ref, sign_ref, had_ref, out_ref, part * span, 2 * quarter + part * span, part * span, pair)
        starts = [half * quarter + part * span for part in range(chunks)]
        join_runs([out_ref] * chunks, starts, out_ref, starts, span, 4)


def join_kernel(low_ref, high_ref, out_ref, *, quarter):
    join_runs([low_ref, low_ref, high_ref, high_ref], [0, quarter] * 2, out_ref, range(0, 4 * quarter, quarter),
              quarter, 8)


def mix_first(slab, signs):
    rows, width = slab.shape
    half = jax.ShapeDtypeStruct((rows // 2, width), jnp.float32)
    return pl.pallas_call(
        functools.partial(mix_first_kernel, quarter=rows // 4),
        in_specs=[pl.BlockSpec(memory_space=pltpu.HBM), pl.BlockSpec(memory_space=pltpu.VMEM)],
        out_specs=[pl.BlockSpec(memory_space=pltpu.VMEM)] * 2,
        out_shape=[half, half],
        scratch_shapes=[
            pltpu.VMEM((TILE, TILE), jnp.bfloat16),
            pltpu.VMEM(half.shape, jnp.float32),
            pltpu.SemaphoreType.DMA((rows // (2 * TILE),)),
        ],
        compiler_params=pltpu.CompilerParams(vmem_limit_bytes=FIRST_LIMIT << 20),
    )(slab, signs)


def mix_next(rest, signs):
    return pl.pallas_call(
        functools.partial(mix_next_kernel, quarter=rest.shape[0] // 2),
        in_specs=[pl.BlockSpec(memory_space=pltpu.VMEM)] * 2,
        out_specs=pl.BlockSpec(memory_space=pltpu.VMEM),
        out_shape=jax.ShapeDtypeStruct(rest.shape, jnp.float32),
        scratch_shapes=[pltpu.VMEM((TILE, TILE), jnp.bfloat16)],
        compiler_params=pltpu.CompilerParams(vmem_limit_bytes=32 << 20),
    )(rest, signs)


def mix_join(low, high):
    rows, width = low.shape
    return pl.pallas_call(
        functools.partial(join_kernel, quarter=rows // 2),
        in_specs=[pl.BlockSpec(memory_space=pltpu.VMEM)] * 2,
        out_specs=pl.BlockSpec(memory_space=pltpu.VMEM),
        out_shape=jax.ShapeDtypeStruct((2 * rows, width), jnp.float32),
        compiler_params=pltpu.CompilerParams(vmem_limit_bytes=32 << 20),
    )(low, high)


def pick_kernel(pick_ref, mixed_ref, keep_ref, send_ref, *, start, count, order, pick_count, groups, norm_scale):
    device = lax.axis_index("rows")
    sub_row = lax.broadcasted_iota(jnp.int32, (SUB, mixed_ref.shape[1]), 0)
    octets = count // SUB
    for out_ref, low_bit in ((send_ref, 1), (keep_ref, 0)):
        @pl.loop(0, groups // 2)
        def _(pair):
            offset = low_bit
            for place, bit in enumerate(reversed(order)):
                offset = offset | ((pair >> place) & 1) << bit
            scale = parity_sign((device ^ offset) & device).astype(jnp.float32) * norm_scale
            for octet in range(octets):
                rows = None
                for sub in range(SUB):
                    index = pick_ref[offset * pick_count + start + octet * SUB + sub]
                    taken = jnp.broadcast_to(mixed_ref[pl.ds(index, 1), :], sub_row.shape)
                    rows = taken if rows is None else jnp.where(sub_row == sub, taken, rows)
                out_at = pl.multiple_of(pair * count + octet * SUB, SUB)
                out_ref[pl.ds(out_at, SUB), :] = rows * scale


def pick_rows(picks, mixed, start, count, order, groups):
    norm_scale = 1.0 / math.sqrt(mixed.shape[0] * groups)
    half = jax.ShapeDtypeStruct((groups // 2 * count, mixed.shape[1]), jnp.float32)
    return pl.pallas_call(
        functools.partial(pick_kernel, start=start, count=count, order=order, pick_count=picks.shape[0] // groups,
                          groups=groups, norm_scale=norm_scale),
        in_specs=[pl.BlockSpec(memory_space=pltpu.SMEM), pl.BlockSpec(memory_space=pltpu.VMEM)],
        out_specs=[pl.BlockSpec(memory_space=pltpu.VMEM)] * 2,
        out_shape=[half, half],
        compiler_params=pltpu.CompilerParams(vmem_limit_bytes=32 << 20),
    )(picks, mixed)


def strip_bits(group):
    return (0, 1, 2) if group == 0 else (0, 2, 1)


def block_groups(tiles):
    pairs = [(i, j) for i in range(tiles) for j in range(i, tiles)]
    return [pairs[:len(pairs) // 2], pairs[len(pairs) // 2:]]


def strip_starts(group, low_bit):
    height = LANES // STRIPS
    mine = lax.axis_index("rows") & (STRIPS - 1)
    order = strip_bits(group)
    starts = []
    for slot in range(STRIPS // 2):
        offset = low_bit | (slot >> 1) << order[1] | (slot & 1) << order[2]
        starts.append(pl.multiple_of((mine ^ offset) * height, height))
    return starts


def gram_kernel(*refs, scale, peers, groups):
    outs = 2 * len(groups)
    pieces, out_refs, (full_ref, gram_ref) = refs[:-outs - 2], refs[-outs - 2:-2], refs[-2:]
    total = full_ref.shape[1]
    width = total // peers
    column = lax.axis_index("cols")
    at = 0
    for run in range(len(pieces) // peers):
        count = pieces[run * peers].shape[0]
        for peer in range(peers):
            first = pl.multiple_of((column ^ peer) * width, width)
            full_ref[at:at + count, pl.ds(first, width)] = pieces[run * peers + peer][...]
        at += count
    for upper in range(total // LANES):
        here = slice(upper * LANES, (upper + 1) * LANES)
        rows = lax.dot_general(full_ref[:, here], full_ref[:, upper * LANES:], (((0,), (0,)), ((), ())),
                               precision=lax.Precision.HIGHEST, preferred_element_type=jnp.float32)
        gram_ref[here, upper * LANES:] = rows * scale
    height = LANES // STRIPS
    for group, pairs in enumerate(groups):
        for low_bit in range(2):
            for slot, strip in enumerate(strip_starts(group, low_bit)):
                for block, (upper, right) in enumerate(pairs):
                    out_refs[2 * group + low_bit][slot, block * height:(block + 1) * height, :] = gram_ref[
                        pl.ds(upper * LANES + strip, height), right * LANES:(right + 1) * LANES]


def partial_gram(pieces, rows, peers, scale):
    total = pieces[0].shape[1] * peers
    groups = block_groups(total // LANES)
    shapes = []
    for pairs in groups:
        shapes += [jax.ShapeDtypeStruct((STRIPS // 2, len(pairs) * (LANES // STRIPS), LANES), jnp.float32)] * 2
    return pl.pallas_call(
        functools.partial(gram_kernel, scale=scale, peers=peers, groups=groups),
        out_shape=shapes,
        scratch_shapes=[pltpu.VMEM((rows, total), jnp.float32), pltpu.VMEM((total, total), jnp.float32)],
        compiler_params=pltpu.CompilerParams(vmem_limit_bytes=16 << 20),
    )(*pieces)


def split_three(value):
    high = value.astype(jnp.bfloat16).astype(jnp.float32)
    rest = value - high
    middle = rest.astype(jnp.bfloat16).astype(jnp.float32)
    return high, middle, rest - middle


def left_terms(value, axis):
    high, middle, low = split_three(value)
    return jnp.concatenate([high, high, middle, high, middle, low], axis=axis).astype(jnp.bfloat16)


def right_terms(value):
    high, middle, low = split_three(value)
    return jnp.concatenate([high, middle, high, low, middle, high], axis=0).astype(jnp.bfloat16)


def times(left, right):
    return jnp.dot(left_terms(left, 1), right_terms(right), preferred_element_type=jnp.float32)


def inner_product(left, right):
    return lax.dot_general(left_terms(left, 0), right_terms(right), (((0,), (0,)), ((), ())),
                           preferred_element_type=jnp.float32)


def lane_splat(value, lane):
    return jnp.broadcast_to(value[:, lane:lane + 1], (value.shape[0], LANES))


def factor_tile(diagonal, column_ref, lead_ref, below_ref):
    row = lax.broadcasted_iota(jnp.int32, (LANES, LANES), 0)
    col = lax.broadcasted_iota(jnp.int32, (LANES, LANES), 1)
    identity = (row == col).astype(jnp.float32)
    whole = jnp.concatenate([diagonal, identity], axis=1)
    slabs = LANES // SUB
    tile = [whole[SUB * t:SUB * t + SUB] for t in range(slabs)]
    sub_row = lax.broadcasted_iota(jnp.int32, tile[0].shape, 0)
    done = []

    def widen(value):
        return jnp.concatenate([value, value], axis=1)

    def splats(slab, at):
        return [lane_splat(tile[slab][:, :LANES], SUB * at + j) for j in range(SUB)]

    own, near = splats(0, 0), splats(1, 0)
    for at in range(slabs):
        lead = tile[at]
        direct = range(at + 1, min(slabs, at + 1 + AHEAD))
        for j in range(SUB):
            column_ref[(at * SUB + j) * SUB:(at * SUB + j + 1) * SUB, :] = own[j]
        for half in range(2):
            lead_ref[half * LANES + at * SUB:half * LANES + (at + 1) * SUB, :] = lead[:, half * LANES:(half + 1) * LANES]
        pivot = {(i, j): column_ref[pl.ds((at * SUB + j) * SUB + i, SUB, stride=0), :]
                 for j in range(SUB) for i in range(j + 1)}
        below = [near if u == at + 1 else splats(u, at) for u in direct]
        if at + 1 < slabs:
            own = splats(at + 1, at + 1)
        if at + 2 < slabs:
            near = splats(at + 2, at + 1)
        rows = [jnp.concatenate([lead_ref[pl.ds(half * LANES + at * SUB + m, SUB, stride=0), :] for half in range(2)],
                                axis=1) for m in range(SUB)]
        panel = jnp.zeros_like(lead)
        for m in range(SUB):
            inverse = lax.rsqrt(pivot[m, m])
            for j in range(m + 1, SUB):
                pivot[m, j] = pivot[m, j] * inverse
            for i in range(m + 1, SUB):
                for j in range(i, SUB):
                    pivot[i, j] = pivot[i, j] - pivot[m, i] * pivot[m, j]
            rows[m] = rows[m] * widen(inverse)
            for j in range(m + 1, SUB):
                rows[j] = rows[j] - widen(pivot[m, j]) * rows[m]
            panel = jnp.where(sub_row == m, rows[m], panel)
            for column, u in zip(below, direct):
                column[m] = column[m] * inverse
                for j in range(m + 1, SUB):
                    column[j] = column[j] - pivot[m, j] * column[m]
                tile[u] = tile[u] - widen(column[m]) * rows[m]
            if below:
                slot = (at * SUB + m) * SUB
                below_ref[slot:slot + SUB, :] = below[0][m]
                for j in range(SUB):
                    spread = below_ref[pl.ds(slot + j, SUB, stride=0), :]
                    own[j] = own[j] - below[0][m] * spread
                    if len(below) > 1:
                        near[j] = near[j] - below[1][m] * spread
        done.append(panel)
        if at + 1 + AHEAD < slabs:
            update = lax.dot_general(left_terms(panel[:, :LANES], 0), right_terms(panel), (((0,), (0,)), ((), ())),
                                     preferred_element_type=jnp.float32)
            for u in range(at + 1 + AHEAD, slabs):
                tile[u] = tile[u] - update[SUB * u:SUB * u + SUB]
    factored = jnp.concatenate(done, axis=0)
    return jnp.where(col >= row, factored[:, :LANES], 0.0), factored[:, LANES:]


def factor_kernel(*refs, groups):
    strip_refs, (out_ref, gram_ref, factor_ref, column_ref, lead_ref, below_ref) = refs[:-6], refs[-6:]
    tiles = gram_ref.shape[0] // LANES
    height = LANES // STRIPS
    for group, pairs in enumerate(groups):
        for low_bit in range(2):
            for slot, strip in enumerate(strip_starts(group, low_bit)):
                for block, (upper, right) in enumerate(pairs):
                    gram_ref[pl.ds(upper * LANES + strip, height), right * LANES:(right + 1) * LANES] = strip_refs[
                        2 * group + low_bit][slot, block * height:(block + 1) * height, :]
    factor_ref[...] = jnp.zeros_like(factor_ref)
    for at in range(tiles):
        here = slice(at * LANES, (at + 1) * LANES)
        factor, inverse = factor_tile(gram_ref[here, here], column_ref, lead_ref, below_ref)
        factor_ref[here, here] = factor
        if at < tiles - 1:
            rest = (at + 1) * LANES
            panel = times(inverse, gram_ref[here, rest:])
            factor_ref[here, rest:] = panel
            gram_ref[rest:, rest:] -= inner_product(panel, panel)
    width = out_ref.shape[1]
    first = pl.multiple_of(lax.axis_index("cols") * width, width)
    out_ref[...] = factor_ref[:, pl.ds(first, width)]


def factor_panel(strips, total, width):
    return pl.pallas_call(
        functools.partial(factor_kernel, groups=block_groups(total // LANES)),
        out_shape=jax.ShapeDtypeStruct((total, width), jnp.float32),
        scratch_shapes=[pltpu.VMEM((total, total), jnp.float32)] * 2 + [
            pltpu.VMEM((LANES * SUB, LANES), jnp.float32), pltpu.VMEM((2 * LANES, LANES), jnp.float32),
            pltpu.VMEM((LANES * SUB, LANES), jnp.float32)],
        compiler_params=pltpu.CompilerParams(vmem_limit_bytes=16 << 20),
    )(*strips)


def summed_strips(keep, send, group, bits):
    core, *order = strip_bits(group)
    gram = keep + swapped(send, "rows", core)
    for bit in order:
        half = gram.shape[0] // 2
        gram = gram[:half] + swapped(gram[half:], "rows", bit)
    for bit in range(len(order) + 1, bits):
        gram = gram + swapped(gram, "rows", bit)
    for bit in reversed(order):
        gram = jnp.concatenate([gram, swapped(gram, "rows", bit)])
    return [gram, swapped(gram, "rows", core)]


def reduce_run(keep, send, order):
    value = keep + swapped(send, "rows", 0)
    for bit in order:
        half = value.shape[0] // 2
        value = value[:half] + swapped(value[half:], "rows", bit)
    return value


def body(slab, sign_bits, block_mask, sample_rows):
    row_count, panel_width = slab.shape
    groups = lax.axis_size("rows")
    peers = lax.axis_size("cols")
    bits = groups.bit_length() - 1
    pick_count = sample_rows.shape[0]
    blocks = block_mask.shape[0]
    signs = (2 * sign_bits - 1).reshape(blocks, row_count // blocks) * block_mask.reshape(blocks, 1)
    signs = signs.reshape(row_count // LANES, LANES).astype(jnp.float32)
    picks = sample_rows
    for bit in range(bits):
        run = bit - (bits - 3)
        if run == 0:
            picks, signs = lax.optimization_barrier((picks, signs))
        other = swapped(picks, "rows", bit)
        if run == 0:
            low, rest = mix_first(slab, signs)
            other, low, rest = lax.optimization_barrier((other, low, rest))
        elif run == 1:
            high = mix_next(rest, signs)
            other, low, high = lax.optimization_barrier((other, low, high))
        elif run == 2:
            mixed = mix_join(low, high)
            other, mixed = lax.optimization_barrier((other, mixed))
        picks = jnp.concatenate([picks, other])
    first = pick_count // 2
    cross = list(range(1, bits))
    sketch = []
    pieces = []
    for start, count, order in ((0, first, cross), (first, pick_count - first, cross[1:2] + cross[:1] + cross[2:])):
        keep, send = pick_rows(picks, mixed, start, count, order, groups)
        part = reduce_run(keep, send, order)
        sketch.append(part)
        pieces.append(part)
        for peer in range(1, peers):
            pieces.append(lax.ppermute(part, "cols", [(i, i ^ peer) for i in range(peers)]))
    sketch = jnp.concatenate(sketch)
    parts = partial_gram(pieces, pick_count, peers, 1.0 / (pick_count * groups))
    strips = []
    for group in range(len(parts) // 2):
        strips += summed_strips(parts[2 * group], parts[2 * group + 1], group, bits)
    r_panel = factor_panel(strips, panel_width * peers, panel_width)
    return (sketch, r_panel)


def solution(mesh):
    in_specs = (P("rows", "cols"), P("rows"), P("rows"), P("rows"))
    out_specs = (P("rows", "cols"), P(None, "cols"))
    return jax.shard_map(body, mesh=mesh, in_specs=in_specs, out_specs=out_specs, check_vma=False)
```

```python
import functools
import math

import jax
import jax.numpy as jnp
from jax import lax
from jax.experimental import pallas as pl
from jax.experimental.pallas import tpu as pltpu
from jax.sharding import PartitionSpec as P

TILE = 256
LANES = 128
SUB = 8
STRIPS = 8
AHEAD = 3
FIRST_LIMIT = 40


def swapped(value, axis, bit):
    return lax.ppermute(value, axis, [(i, i ^ 1 << bit) for i in range(lax.axis_size(axis))])


def parity_sign(common):
    for shift in (16, 8, 4, 2, 1):
        common = common ^ (common >> shift)
    return 1 - 2 * (common & 1)


def butterfly(parts):
    stride = 1
    while stride < len(parts):
        for at in range(len(parts)):
            if at & stride == 0:
                low, high = parts[at], parts[at + stride]
                parts[at], parts[at + stride] = low + high, low - high
        stride *= 2
    return parts


def split_two(value):
    high = value.astype(jnp.bfloat16)
    low = (value - high.astype(jnp.float32)).astype(jnp.bfloat16)
    return high, low


def fill_hadamard(had_ref):
    row = lax.broadcasted_iota(jnp.int32, (TILE, TILE), 0)
    col = lax.broadcasted_iota(jnp.int32, (TILE, TILE), 1)
    had_ref[...] = parity_sign(row & col).astype(jnp.float32).astype(jnp.bfloat16)


def mix_tiles(source_ref, sign_ref, had_ref, out_ref, source_at, sign_at, out_at, count):
    per_tile = TILE // LANES
    mixed = []
    for block in range(count):
        signed = []
        for half in range(per_tile):
            at = sign_at // LANES + block * per_tile + half
            sign = sign_ref[at:at + 1, :].astype(jnp.bfloat16)
            signed.append(had_ref[:, half * LANES:(half + 1) * LANES] * sign)
        left = jnp.concatenate(signed * 2, axis=1)
        part = source_ref[source_at + block * TILE:source_at + (block + 1) * TILE, :]
        right = jnp.concatenate(split_two(part), axis=0)
        mixed.append(jnp.dot(left, right, preferred_element_type=jnp.float32))
    mixed = butterfly(mixed)
    for block in range(count):
        at = out_at + block * TILE
        out_ref[at:at + TILE, :] = mixed[block]


def join_runs(refs, starts, out_ref, out_starts, rows, unroll):
    @pl.loop(0, rows // (SUB * unroll))
    def _(batch):
        for sub in range(unroll):
            base = pl.multiple_of(batch * SUB * unroll, SUB * unroll) + sub * SUB
            values = butterfly([ref[pl.ds(start + base, SUB), :] for ref, start in zip(refs, starts)])
            for start, value in zip(out_starts, values):
                out_ref[pl.ds(start + base, SUB), :] = value


def mix_first_kernel(slab_ref, sign_ref, out_ref, rest_ref, had_ref, buf_ref, sems, *, quarter):
    pair = 2
    span = pair * TILE
    chunks = quarter // span

    def fetch(part):
        rows = pl.ds(part * span, span)
        if part < 2 * chunks:
            target = buf_ref.at[rows, :]
        else:
            target = rest_ref.at[pl.ds((part - 2 * chunks) * span, span), :]
        return pltpu.make_async_copy(slab_ref.at[rows, :], target, sems.at[part])

    for part in range(4 * chunks):
        fetch(part).start()
    fill_hadamard(had_ref)
    for half in range(2):
        for part in range(half * chunks, (half + 1) * chunks):
            fetch(part).wait()
            mix_tiles(buf_ref, sign_ref, had_ref, out_ref, part * span, part * span, part * span, pair)
        starts = [half * quarter + at * span for at in range(chunks)]
        join_runs([out_ref] * chunks, starts, out_ref, starts, span, 4)
    for part in range(2 * chunks, 4 * chunks):
        fetch(part).wait()


def mix_next_kernel(rest_ref, sign_ref, out_ref, had_ref, *, quarter):
    pair = 2
    span = pair * TILE
    chunks = quarter // span
    fill_hadamard(had_ref)
    for half in range(2):
        for part in range(half * chunks, (half + 1) * chunks):
            mix_tiles(rest_ref, sign_ref, had_ref, out_ref, part * span, 2 * quarter + part * span, part * span, pair)
        starts = [half * quarter + part * span for part in range(chunks)]
        join_runs([out_ref] * chunks, starts, out_ref, starts, span, 4)


def join_kernel(low_ref, high_ref, out_ref, *, quarter):
    join_runs([low_ref, low_ref, high_ref, high_ref], [0, quarter] * 2, out_ref, range(0, 4 * quarter, quarter),
              quarter, 8)


def mix_first(slab, signs):
    rows, width = slab.shape
    half = jax.ShapeDtypeStruct((rows // 2, width), jnp.float32)
    return pl.pallas_call(
        functools.partial(mix_first_kernel, quarter=rows // 4),
        in_specs=[pl.BlockSpec(memory_space=pltpu.HBM), pl.BlockSpec(memory_space=pltpu.VMEM)],
        out_specs=[pl.BlockSpec(memory_space=pltpu.VMEM)] * 2,
        out_shape=[half, half],
        scratch_shapes=[
            pltpu.VMEM((TILE, TILE), jnp.bfloat16),
            pltpu.VMEM(half.shape, jnp.float32),
            pltpu.SemaphoreType.DMA((rows // (2 * TILE),)),
        ],
        compiler_params=pltpu.CompilerParams(vmem_limit_bytes=FIRST_LIMIT << 20),
    )(slab, signs)


def mix_next(rest, signs):
    return pl.pallas_call(
        functools.partial(mix_next_kernel, quarter=rest.shape[0] // 2),
        in_specs=[pl.BlockSpec(memory_space=pltpu.VMEM)] * 2,
        out_specs=pl.BlockSpec(memory_space=pltpu.VMEM),
        out_shape=jax.ShapeDtypeStruct(rest.shape, jnp.float32),
        scratch_shapes=[pltpu.VMEM((TILE, TILE), jnp.bfloat16)],
        compiler_params=pltpu.CompilerParams(vmem_limit_bytes=32 << 20),
    )(rest, signs)


def mix_join(low, high):
    rows, width = low.shape
    return pl.pallas_call(
        functools.partial(join_kernel, quarter=rows // 2),
        in_specs=[pl.BlockSpec(memory_space=pltpu.VMEM)] * 2,
        out_specs=pl.BlockSpec(memory_space=pltpu.VMEM),
        out_shape=jax.ShapeDtypeStruct((2 * rows, width), jnp.float32),
        compiler_params=pltpu.CompilerParams(vmem_limit_bytes=32 << 20),
    )(low, high)


def pick_kernel(pick_ref, mixed_ref, keep_ref, send_ref, *, start, count, order, pick_count, groups, norm_scale):
    device = lax.axis_index("rows")
    sub_row = lax.broadcasted_iota(jnp.int32, (SUB, mixed_ref.shape[1]), 0)
    octets = count // SUB
    for out_ref, low_bit in ((send_ref, 1), (keep_ref, 0)):
        @pl.loop(0, groups // 2)
        def _(pair):
            offset = low_bit
            for place, bit in enumerate(reversed(order)):
                offset = offset | ((pair >> place) & 1) << bit
            scale = parity_sign((device ^ offset) & device).astype(jnp.float32) * norm_scale
            for octet in range(octets):
                rows = None
                for sub in range(SUB):
                    index = pick_ref[offset * pick_count + start + octet * SUB + sub]
                    taken = jnp.broadcast_to(mixed_ref[pl.ds(index, 1), :], sub_row.shape)
                    rows = taken if rows is None else jnp.where(sub_row == sub, taken, rows)
                out_at = pl.multiple_of(pair * count + octet * SUB, SUB)
                out_ref[pl.ds(out_at, SUB), :] = rows * scale


def pick_rows(picks, mixed, start, count, order, groups):
    norm_scale = 1.0 / math.sqrt(mixed.shape[0] * groups)
    half = jax.ShapeDtypeStruct((groups // 2 * count, mixed.shape[1]), jnp.float32)
    return pl.pallas_call(
        functools.partial(pick_kernel, start=start, count=count, order=order, pick_count=picks.shape[0] // groups,
                          groups=groups, norm_scale=norm_scale),
        in_specs=[pl.BlockSpec(memory_space=pltpu.SMEM), pl.BlockSpec(memory_space=pltpu.VMEM)],
        out_specs=[pl.BlockSpec(memory_space=pltpu.VMEM)] * 2,
        out_shape=[half, half],
        compiler_params=pltpu.CompilerParams(vmem_limit_bytes=32 << 20),
    )(picks, mixed)


def strip_bits(group):
    return (0, 1, 2) if group == 0 else (0, 2, 1)


def own_pairs(tiles):
    return [(i, j) for i in range(tiles) for j in range(i, tiles)]


def cross_pairs(tiles, peers):
    total = tiles * peers
    return [(i, j) for i in range(total) for j in range(i, total) if i // tiles != j // tiles]


def strip_starts(group, low_bit):
    height = LANES // STRIPS
    mine = lax.axis_index("rows") & (STRIPS - 1)
    order = strip_bits(group)
    starts = []
    for slot in range(STRIPS // 2):
        offset = low_bit | (slot >> 1) << order[1] | (slot & 1) << order[2]
        starts.append(pl.multiple_of((mine ^ offset) * height, height))
    return starts


def gram_kernel(*refs, scale, peers, pairs, group):
    pieces, (keep_ref, send_ref, full_ref, gram_ref) = refs[:-4], refs[-4:]
    total = full_ref.shape[1]
    width = total // peers
    at = 0
    for run in range(len(pieces) // peers):
        count = pieces[run * peers].shape[0]
        for peer in range(peers):
            first = pl.multiple_of((lax.axis_index("cols") ^ peer) * width, width) if peers > 1 else 0
            full_ref[at:at + count, pl.ds(first, width)] = pieces[run * peers + peer][...]
        at += count
    for upper in sorted({i for i, _ in pairs}):
        here = slice(upper * LANES, (upper + 1) * LANES)
        left = min(j for i, j in pairs if i == upper) * LANES
        rows = lax.dot_general(full_ref[:, here], full_ref[:, left:], (((0,), (0,)), ((), ())),
                               precision=lax.Precision.HIGHEST, preferred_element_type=jnp.float32)
        gram_ref[here, left:] = rows * scale
    height = LANES // STRIPS
    for low_bit, out_ref in ((0, keep_ref), (1, send_ref)):
        for slot, strip in enumerate(strip_starts(group, low_bit)):
            for block, (upper, right) in enumerate(pairs):
                out_ref[slot, block * height:(block + 1) * height, :] = gram_ref[
                    pl.ds(upper * LANES + strip, height), right * LANES:(right + 1) * LANES]


def partial_gram(pieces, rows, peers, pairs, group, scale):
    total = pieces[0].shape[1] * peers
    half = jax.ShapeDtypeStruct((STRIPS // 2, len(pairs) * (LANES // STRIPS), LANES), jnp.float32)
    return pl.pallas_call(
        functools.partial(gram_kernel, scale=scale, peers=peers, pairs=pairs, group=group),
        out_shape=[half, half],
        scratch_shapes=[pltpu.VMEM((rows, total), jnp.float32), pltpu.VMEM((total, total), jnp.float32)],
        compiler_params=pltpu.CompilerParams(vmem_limit_bytes=16 << 20),
    )(*pieces)


def split_three(value):
    high = value.astype(jnp.bfloat16).astype(jnp.float32)
    rest = value - high
    middle = rest.astype(jnp.bfloat16).astype(jnp.float32)
    return high, middle, rest - middle


def left_terms(value, axis):
    high, middle, low = split_three(value)
    return jnp.concatenate([high, high, middle, high, middle, low], axis=axis).astype(jnp.bfloat16)


def right_terms(value):
    high, middle, low = split_three(value)
    return jnp.concatenate([high, middle, high, low, middle, high], axis=0).astype(jnp.bfloat16)


def times(left, right):
    return jnp.dot(left_terms(left, 1), right_terms(right), preferred_element_type=jnp.float32)


def inner_product(left, right):
    return lax.dot_general(left_terms(left, 0), right_terms(right), (((0,), (0,)), ((), ())),
                           preferred_element_type=jnp.float32)


def lane_splat(value, lane):
    return jnp.broadcast_to(value[:, lane:lane + 1], (value.shape[0], LANES))


def factor_tile(diagonal, column_ref, lead_ref, below_ref):
    row = lax.broadcasted_iota(jnp.int32, (LANES, LANES), 0)
    col = lax.broadcasted_iota(jnp.int32, (LANES, LANES), 1)
    identity = (row == col).astype(jnp.float32)
    whole = jnp.concatenate([diagonal, identity], axis=1)
    slabs = LANES // SUB
    tile = [whole[SUB * t:SUB * t + SUB] for t in range(slabs)]
    sub_row = lax.broadcasted_iota(jnp.int32, tile[0].shape, 0)
    done = []

    def widen(value):
        return jnp.concatenate([value, value], axis=1)

    def splats(slab, at):
        return [lane_splat(tile[slab][:, :LANES], SUB * at + j) for j in range(SUB)]

    own, near = splats(0, 0), splats(1, 0)
    for at in range(slabs):
        lead = tile[at]
        direct = range(at + 1, min(slabs, at + 1 + AHEAD))
        for j in range(SUB):
            column_ref[(at * SUB + j) * SUB:(at * SUB + j + 1) * SUB, :] = own[j]
        for half in range(2):
            lead_ref[half * LANES + at * SUB:half * LANES + (at + 1) * SUB, :] = lead[:, half * LANES:(half + 1) * LANES]
        pivot = {(i, j): column_ref[pl.ds((at * SUB + j) * SUB + i, SUB, stride=0), :]
                 for j in range(SUB) for i in range(j + 1)}
        below = [near if u == at + 1 else splats(u, at) for u in direct]
        if at + 1 < slabs:
            own = splats(at + 1, at + 1)
        if at + 2 < slabs:
            near = splats(at + 2, at + 1)
        rows = [jnp.concatenate([lead_ref[pl.ds(half * LANES + at * SUB + m, SUB, stride=0), :] for half in range(2)],
                                axis=1) for m in range(SUB)]
        panel = jnp.zeros_like(lead)
        for m in range(SUB):
            inverse = lax.rsqrt(pivot[m, m])
            for j in range(m + 1, SUB):
                pivot[m, j] = pivot[m, j] * inverse
            for i in range(m + 1, SUB):
                for j in range(i, SUB):
                    pivot[i, j] = pivot[i, j] - pivot[m, i] * pivot[m, j]
            rows[m] = rows[m] * widen(inverse)
            for j in range(m + 1, SUB):
                rows[j] = rows[j] - widen(pivot[m, j]) * rows[m]
            panel = jnp.where(sub_row == m, rows[m], panel)
            for column, u in zip(below, direct):
                column[m] = column[m] * inverse
                for j in range(m + 1, SUB):
                    column[j] = column[j] - pivot[m, j] * column[m]
                tile[u] = tile[u] - widen(column[m]) * rows[m]
            if below:
                slot = (at * SUB + m) * SUB
                below_ref[slot:slot + SUB, :] = below[0][m]
                for j in range(SUB):
                    spread = below_ref[pl.ds(slot + j, SUB, stride=0), :]
                    own[j] = own[j] - below[0][m] * spread
                    if len(below) > 1:
                        near[j] = near[j] - below[1][m] * spread
        done.append(panel)
        if at + 1 + AHEAD < slabs:
            update = lax.dot_general(left_terms(panel[:, :LANES], 0), right_terms(panel), (((0,), (0,)), ((), ())),
                                     preferred_element_type=jnp.float32)
            for u in range(at + 1 + AHEAD, slabs):
                tile[u] = tile[u] - update[SUB * u:SUB * u + SUB]
    factored = jnp.concatenate(done, axis=0)
    return jnp.where(col >= row, factored[:, :LANES], 0.0), factored[:, LANES:]


def factor_kernel(*refs, peers):
    strip_refs, (out_ref, gram_ref, factor_ref, column_ref, lead_ref, below_ref) = refs[:-6], refs[-6:]
    tiles = gram_ref.shape[0] // LANES
    panel_tiles = tiles // peers
    height = LANES // STRIPS
    own = own_pairs(panel_tiles)
    for low_bit in range(2):
        for slot, strip in enumerate(strip_starts(0, low_bit)):
            for peer in range(peers):
                base = (lax.axis_index("cols") ^ peer) * (panel_tiles * LANES)
                for block, (upper, right) in enumerate(own):
                    at = (peer * len(own) + block) * height
                    gram_ref[pl.ds(pl.multiple_of(base + upper * LANES + strip, height), height),
                             pl.ds(pl.multiple_of(base + right * LANES, LANES), LANES)] = strip_refs[low_bit][
                        slot, at:at + height, :]
        for slot, strip in enumerate(strip_starts(1, low_bit)):
            for block, (upper, right) in enumerate(cross_pairs(panel_tiles, peers)):
                gram_ref[pl.ds(upper * LANES + strip, height), right * LANES:(right + 1) * LANES] = strip_refs[
                    2 + low_bit][slot, block * height:(block + 1) * height, :]
    factor_ref[...] = jnp.zeros_like(factor_ref)
    for at in range(tiles):
        here = slice(at * LANES, (at + 1) * LANES)
        factor, inverse = factor_tile(gram_ref[here, here], column_ref, lead_ref, below_ref)
        factor_ref[here, here] = factor
        if at < tiles - 1:
            rest = (at + 1) * LANES
            panel = times(inverse, gram_ref[here, rest:])
            factor_ref[here, rest:] = panel
            gram_ref[rest:, rest:] -= inner_product(panel, panel)
    width = out_ref.shape[1]
    first = pl.multiple_of(lax.axis_index("cols") * width, width)
    out_ref[...] = factor_ref[:, pl.ds(first, width)]


def factor_panel(strips, peers, width):
    total = width * peers
    return pl.pallas_call(
        functools.partial(factor_kernel, peers=peers),
        out_shape=jax.ShapeDtypeStruct((total, width), jnp.float32),
        scratch_shapes=[pltpu.VMEM((total, total), jnp.float32)] * 2 + [
            pltpu.VMEM((LANES * SUB, LANES), jnp.float32), pltpu.VMEM((2 * LANES, LANES), jnp.float32),
            pltpu.VMEM((LANES * SUB, LANES), jnp.float32)],
        compiler_params=pltpu.CompilerParams(vmem_limit_bytes=16 << 20),
    )(*strips)


def summed_strips(keep, send, group, bits, peers):
    core, *order = strip_bits(group)
    gram = keep + swapped(send, "rows", core)
    for bit in order:
        half = gram.shape[0] // 2
        gram = gram[:half] + swapped(gram[half:], "rows", bit)
    for bit in range(len(order) + 1, bits):
        gram = gram + swapped(gram, "rows", bit)
    others = [lax.ppermute(gram, "cols", [(i, i ^ peer) for i in range(lax.axis_size("cols"))])
              for peer in range(1, peers)]
    gram = jnp.concatenate([gram, *others], axis=1)
    for bit in reversed(order):
        gram = jnp.concatenate([gram, swapped(gram, "rows", bit)])
    return [gram, swapped(gram, "rows", core)]


def reduce_run(keep, send, order):
    value = keep + swapped(send, "rows", 0)
    for bit in order:
        half = value.shape[0] // 2
        value = value[:half] + swapped(value[half:], "rows", bit)
    return value


def body(slab, sign_bits, block_mask, sample_rows):
    row_count, panel_width = slab.shape
    groups = lax.axis_size("rows")
    peers = lax.axis_size("cols")
    bits = groups.bit_length() - 1
    pick_count = sample_rows.shape[0]
    blocks = block_mask.shape[0]
    signs = (2 * sign_bits - 1).reshape(blocks, row_count // blocks) * block_mask.reshape(blocks, 1)
    signs = signs.reshape(row_count // LANES, LANES).astype(jnp.float32)
    picks = sample_rows
    for bit in range(bits):
        run = bit - (bits - 3)
        if run == 0:
            picks, signs = lax.optimization_barrier((picks, signs))
        other = swapped(picks, "rows", bit)
        if run == 0:
            low, rest = mix_first(slab, signs)
            other, low, rest = lax.optimization_barrier((other, low, rest))
        elif run == 1:
            high = mix_next(rest, signs)
            other, low, high = lax.optimization_barrier((other, low, high))
        elif run == 2:
            mixed = mix_join(low, high)
            other, mixed = lax.optimization_barrier((other, mixed))
        picks = jnp.concatenate([picks, other])
    first = pick_count // 2
    cross = list(range(1, bits))
    parts = []
    pieces = []
    for start, count, order in ((0, first, cross), (first, pick_count - first, cross[1:2] + cross[:1] + cross[2:])):
        keep, send = pick_rows(picks, mixed, start, count, order, groups)
        part = reduce_run(keep, send, order)
        parts.append(part)
        pieces.append(part)
        for peer in range(1, peers):
            pieces.append(lax.ppermute(part, "cols", [(i, i ^ peer) for i in range(peers)]))
    sketch = jnp.concatenate(parts)
    tiles = panel_width // LANES
    scale = 1.0 / (pick_count * groups)
    own = partial_gram(parts, pick_count, 1, own_pairs(tiles), 0, scale)
    cross = partial_gram(pieces, pick_count, peers, cross_pairs(tiles, peers), 1, scale)
    strips = summed_strips(*own, 0, bits, peers) + summed_strips(*cross, 1, bits, 1)
    r_panel = factor_panel(strips, peers, panel_width)
    return (sketch, r_panel)


def solution(mesh):
    in_specs = (P("rows", "cols"), P("rows"), P("rows"), P("rows"))
    out_specs = (P("rows", "cols"), P(None, "cols"))
    return jax.shard_map(body, mesh=mesh, in_specs=in_specs, out_specs=out_specs, check_vma=False)
```

```python
import functools
import math

import jax
import jax.numpy as jnp
from jax import lax
from jax.experimental import pallas as pl
from jax.experimental.pallas import tpu as pltpu
from jax.sharding import PartitionSpec as P

TILE = 256
LANES = 128
SUB = 8
STRIPS = 8
AHEAD = 3
FIRST_LIMIT = 40


def swapped(value, axis, bit):
    return lax.ppermute(value, axis, [(i, i ^ 1 << bit) for i in range(lax.axis_size(axis))])


def parity_sign(common):
    for shift in (16, 8, 4, 2, 1):
        common = common ^ (common >> shift)
    return 1 - 2 * (common & 1)


def butterfly(parts):
    stride = 1
    while stride < len(parts):
        for at in range(len(parts)):
            if at & stride == 0:
                low, high = parts[at], parts[at + stride]
                parts[at], parts[at + stride] = low + high, low - high
        stride *= 2
    return parts


def split_two(value):
    high = value.astype(jnp.bfloat16)
    low = (value - high.astype(jnp.float32)).astype(jnp.bfloat16)
    return high, low


def fill_hadamard(had_ref):
    row = lax.broadcasted_iota(jnp.int32, (TILE, TILE), 0)
    col = lax.broadcasted_iota(jnp.int32, (TILE, TILE), 1)
    had_ref[...] = parity_sign(row & col).astype(jnp.float32).astype(jnp.bfloat16)


def mix_tiles(source_ref, sign_ref, had_ref, out_ref, source_at, sign_at, out_at, count):
    per_tile = TILE // LANES
    mixed = []
    for block in range(count):
        signed = []
        for half in range(per_tile):
            at = sign_at // LANES + block * per_tile + half
            sign = sign_ref[at:at + 1, :].astype(jnp.bfloat16)
            signed.append(had_ref[:, half * LANES:(half + 1) * LANES] * sign)
        left = jnp.concatenate(signed * 2, axis=1)
        part = source_ref[source_at + block * TILE:source_at + (block + 1) * TILE, :]
        right = jnp.concatenate(split_two(part), axis=0)
        mixed.append(jnp.dot(left, right, preferred_element_type=jnp.float32))
    mixed = butterfly(mixed)
    for block in range(count):
        at = out_at + block * TILE
        out_ref[at:at + TILE, :] = mixed[block]


def join_runs(refs, starts, out_ref, out_starts, rows, unroll):
    @pl.loop(0, rows // (SUB * unroll))
    def _(batch):
        for sub in range(unroll):
            base = pl.multiple_of(batch * SUB * unroll, SUB * unroll) + sub * SUB
            values = butterfly([ref[pl.ds(start + base, SUB), :] for ref, start in zip(refs, starts)])
            for start, value in zip(out_starts, values):
                out_ref[pl.ds(start + base, SUB), :] = value


def mix_first_kernel(slab_ref, sign_ref, out_ref, rest_ref, had_ref, buf_ref, sems, *, quarter):
    pair = 2
    span = pair * TILE
    chunks = quarter // span

    def fetch(part):
        rows = pl.ds(part * span, span)
        if part < 2 * chunks:
            target = buf_ref.at[rows, :]
        else:
            target = rest_ref.at[pl.ds((part - 2 * chunks) * span, span), :]
        return pltpu.make_async_copy(slab_ref.at[rows, :], target, sems.at[part])

    for part in range(4 * chunks):
        fetch(part).start()
    fill_hadamard(had_ref)
    for half in range(2):
        for part in range(half * chunks, (half + 1) * chunks):
            fetch(part).wait()
            mix_tiles(buf_ref, sign_ref, had_ref, out_ref, part * span, part * span, part * span, pair)
        starts = [half * quarter + at * span for at in range(chunks)]
        join_runs([out_ref] * chunks, starts, out_ref, starts, span, 4)
    for part in range(2 * chunks, 4 * chunks):
        fetch(part).wait()


def mix_next_kernel(rest_ref, sign_ref, out_ref, had_ref, *, quarter):
    pair = 2
    span = pair * TILE
    chunks = quarter // span
    fill_hadamard(had_ref)
    for half in range(2):
        for part in range(half * chunks, (half + 1) * chunks):
            mix_tiles(rest_ref, sign_ref, had_ref, out_ref, part * span, 2 * quarter + part * span, part * span, pair)
        starts = [half * quarter + part * span for part in range(chunks)]
        join_runs([out_ref] * chunks, starts, out_ref, starts, span, 4)


def join_kernel(low_ref, high_ref, out_ref, *, quarter):
    join_runs([low_ref, low_ref, high_ref, high_ref], [0, quarter] * 2, out_ref, range(0, 4 * quarter, quarter),
              quarter, 8)


def mix_first(slab, signs):
    rows, width = slab.shape
    half = jax.ShapeDtypeStruct((rows // 2, width), jnp.float32)
    return pl.pallas_call(
        functools.partial(mix_first_kernel, quarter=rows // 4),
        in_specs=[pl.BlockSpec(memory_space=pltpu.HBM), pl.BlockSpec(memory_space=pltpu.VMEM)],
        out_specs=[pl.BlockSpec(memory_space=pltpu.VMEM)] * 2,
        out_shape=[half, half],
        scratch_shapes=[
            pltpu.VMEM((TILE, TILE), jnp.bfloat16),
            pltpu.VMEM(half.shape, jnp.float32),
            pltpu.SemaphoreType.DMA((rows // (2 * TILE),)),
        ],
        compiler_params=pltpu.CompilerParams(vmem_limit_bytes=FIRST_LIMIT << 20),
    )(slab, signs)


def mix_next(rest, signs):
    return pl.pallas_call(
        functools.partial(mix_next_kernel, quarter=rest.shape[0] // 2),
        in_specs=[pl.BlockSpec(memory_space=pltpu.VMEM)] * 2,
        out_specs=pl.BlockSpec(memory_space=pltpu.VMEM),
        out_shape=jax.ShapeDtypeStruct(rest.shape, jnp.float32),
        scratch_shapes=[pltpu.VMEM((TILE, TILE), jnp.bfloat16)],
        compiler_params=pltpu.CompilerParams(vmem_limit_bytes=32 << 20),
    )(rest, signs)


def mix_join(low, high):
    rows, width = low.shape
    return pl.pallas_call(
        functools.partial(join_kernel, quarter=rows // 2),
        in_specs=[pl.BlockSpec(memory_space=pltpu.VMEM)] * 2,
        out_specs=pl.BlockSpec(memory_space=pltpu.VMEM),
        out_shape=jax.ShapeDtypeStruct((2 * rows, width), jnp.float32),
        compiler_params=pltpu.CompilerParams(vmem_limit_bytes=32 << 20),
    )(low, high)


def pick_kernel(pick_ref, mixed_ref, *out_refs, jobs, pick_count, groups, norm_scale):
    device = lax.axis_index("rows")
    sub_row = lax.broadcasted_iota(jnp.int32, (SUB, mixed_ref.shape[1]), 0)

    def pick(out_ref, start, count, order, low_bit):
        @pl.loop(0, groups // 2)
        def _(pair):
            offset = low_bit
            for place, bit in enumerate(reversed(order)):
                offset = offset | ((pair >> place) & 1) << bit
            scale = parity_sign((device ^ offset) & device).astype(jnp.float32) * norm_scale
            for octet in range(count // SUB):
                rows = None
                for sub in range(SUB):
                    index = pick_ref[offset * pick_count + start + octet * SUB + sub]
                    taken = jnp.broadcast_to(mixed_ref[pl.ds(index, 1), :], sub_row.shape)
                    rows = taken if rows is None else jnp.where(sub_row == sub, taken, rows)
                out_at = pl.multiple_of(pair * count + octet * SUB, SUB)
                out_ref[pl.ds(out_at, SUB), :] = rows * scale

    for out_ref, job in zip(out_refs, jobs):
        pick(out_ref, *job)


def pick_rows(picks, mixed, jobs, groups):
    norm_scale = 1.0 / math.sqrt(mixed.shape[0] * groups)
    return pl.pallas_call(
        functools.partial(pick_kernel, jobs=jobs, pick_count=picks.shape[0] // groups,
                          groups=groups, norm_scale=norm_scale),
        in_specs=[pl.BlockSpec(memory_space=pltpu.SMEM), pl.BlockSpec(memory_space=pltpu.VMEM)],
        out_specs=[pl.BlockSpec(memory_space=pltpu.VMEM)] * len(jobs),
        out_shape=[jax.ShapeDtypeStruct((groups // 2 * job[1], mixed.shape[1]), jnp.float32) for job in jobs],
        compiler_params=pltpu.CompilerParams(vmem_limit_bytes=32 << 20),
    )(picks, mixed)


def strip_bits(group):
    return (0, 1, 2) if group == 0 else (0, 2, 1)


def block_groups(tiles):
    pairs = [(i, j) for i in range(tiles) for j in range(i, tiles)]
    return [pairs[:len(pairs) // 2], pairs[len(pairs) // 2:]]


def strip_starts(group, low_bit):
    height = LANES // STRIPS
    mine = lax.axis_index("rows") & (STRIPS - 1)
    order = strip_bits(group)
    starts = []
    for slot in range(STRIPS // 2):
        offset = low_bit | (slot >> 1) << order[1] | (slot & 1) << order[2]
        starts.append(pl.multiple_of((mine ^ offset) * height, height))
    return starts


def gram_kernel(*refs, scale, peers, groups):
    outs = 2 * len(groups)
    pieces, out_refs, (full_ref, gram_ref) = refs[:-outs - 2], refs[-outs - 2:-2], refs[-2:]
    total = full_ref.shape[1]
    width = total // peers
    column = lax.axis_index("cols")
    at = 0
    for run in range(len(pieces) // peers):
        count = pieces[run * peers].shape[0]
        for peer in range(peers):
            first = pl.multiple_of((column ^ peer) * width, width)
            full_ref[at:at + count, pl.ds(first, width)] = pieces[run * peers + peer][...]
        at += count
    for upper in range(total // LANES):
        here = slice(upper * LANES, (upper + 1) * LANES)
        rows = lax.dot_general(full_ref[:, here], full_ref[:, upper * LANES:], (((0,), (0,)), ((), ())),
                               precision=lax.Precision.HIGHEST, preferred_element_type=jnp.float32)
        gram_ref[here, upper * LANES:] = rows * scale
    height = LANES // STRIPS
    for group, pairs in enumerate(groups):
        for low_bit in range(2):
            for slot, strip in enumerate(strip_starts(group, low_bit)):
                for block, (upper, right) in enumerate(pairs):
                    out_refs[2 * group + low_bit][slot, block * height:(block + 1) * height, :] = gram_ref[
                        pl.ds(upper * LANES + strip, height), right * LANES:(right + 1) * LANES]


def partial_gram(pieces, rows, peers, scale):
    total = pieces[0].shape[1] * peers
    groups = block_groups(total // LANES)
    shapes = []
    for pairs in groups:
        shapes += [jax.ShapeDtypeStruct((STRIPS // 2, len(pairs) * (LANES // STRIPS), LANES), jnp.float32)] * 2
    return pl.pallas_call(
        functools.partial(gram_kernel, scale=scale, peers=peers, groups=groups),
        out_shape=shapes,
        scratch_shapes=[pltpu.VMEM((rows, total), jnp.float32), pltpu.VMEM((total, total), jnp.float32)],
        compiler_params=pltpu.CompilerParams(vmem_limit_bytes=16 << 20),
    )(*pieces)


def split_three(value):
    high = value.astype(jnp.bfloat16).astype(jnp.float32)
    rest = value - high
    middle = rest.astype(jnp.bfloat16).astype(jnp.float32)
    return high, middle, rest - middle


def left_terms(value, axis):
    high, middle, low = split_three(value)
    return jnp.concatenate([high, high, middle, high, middle, low], axis=axis).astype(jnp.bfloat16)


def right_terms(value):
    high, middle, low = split_three(value)
    return jnp.concatenate([high, middle, high, low, middle, high], axis=0).astype(jnp.bfloat16)


def times(left, right):
    return jnp.dot(left_terms(left, 1), right_terms(right), preferred_element_type=jnp.float32)


def inner_product(left, right):
    return lax.dot_general(left_terms(left, 0), right_terms(right), (((0,), (0,)), ((), ())),
                           preferred_element_type=jnp.float32)


def lane_splat(value, lane):
    return jnp.broadcast_to(value[:, lane:lane + 1], (value.shape[0], LANES))


def factor_tile(diagonal, column_ref, lead_ref, below_ref, inverted):
    row = lax.broadcasted_iota(jnp.int32, (LANES, LANES), 0)
    col = lax.broadcasted_iota(jnp.int32, (LANES, LANES), 1)
    identity = (row == col).astype(jnp.float32)
    whole = jnp.concatenate([diagonal, identity], axis=1) if inverted else diagonal
    copies = whole.shape[1] // LANES
    slabs = LANES // SUB
    tile = [whole[SUB * t:SUB * t + SUB] for t in range(slabs)]
    sub_row = lax.broadcasted_iota(jnp.int32, tile[0].shape, 0)
    done = []

    def widen(value):
        return jnp.concatenate([value] * copies, axis=1)

    def splats(slab, at):
        return [lane_splat(tile[slab][:, :LANES], SUB * at + j) for j in range(SUB)]

    own, near = splats(0, 0), splats(1, 0)
    for at in range(slabs):
        lead = tile[at]
        direct = range(at + 1, min(slabs, at + 1 + AHEAD))
        for j in range(SUB):
            column_ref[(at * SUB + j) * SUB:(at * SUB + j + 1) * SUB, :] = own[j]
        for half in range(copies):
            lead_ref[half * LANES + at * SUB:half * LANES + (at + 1) * SUB, :] = lead[:, half * LANES:(half + 1) * LANES]
        pivot = {(i, j): column_ref[pl.ds((at * SUB + j) * SUB + i, SUB, stride=0), :]
                 for j in range(SUB) for i in range(j + 1)}
        below = [near if u == at + 1 else splats(u, at) for u in direct]
        if at + 1 < slabs:
            own = splats(at + 1, at + 1)
        if at + 2 < slabs:
            near = splats(at + 2, at + 1)
        rows = [jnp.concatenate([lead_ref[pl.ds(half * LANES + at * SUB + m, SUB, stride=0), :] for half in range(copies)],
                                axis=1) for m in range(SUB)]
        panel = jnp.zeros_like(lead)
        for m in range(SUB):
            inverse = lax.rsqrt(pivot[m, m])
            for j in range(m + 1, SUB):
                pivot[m, j] = pivot[m, j] * inverse
            for i in range(m + 1, SUB):
                for j in range(i, SUB):
                    pivot[i, j] = pivot[i, j] - pivot[m, i] * pivot[m, j]
            rows[m] = rows[m] * widen(inverse)
            for j in range(m + 1, SUB):
                rows[j] = rows[j] - widen(pivot[m, j]) * rows[m]
            panel = jnp.where(sub_row == m, rows[m], panel)
            for column, u in zip(below, direct):
                column[m] = column[m] * inverse
                for j in range(m + 1, SUB):
                    column[j] = column[j] - pivot[m, j] * column[m]
                tile[u] = tile[u] - widen(column[m]) * rows[m]
            if below:
                slot = (at * SUB + m) * SUB
                below_ref[slot:slot + SUB, :] = below[0][m]
                for j in range(SUB):
                    spread = below_ref[pl.ds(slot + j, SUB, stride=0), :]
                    own[j] = own[j] - below[0][m] * spread
                    if len(below) > 1:
                        near[j] = near[j] - below[1][m] * spread
        done.append(panel)
        if at + 1 + AHEAD < slabs:
            update = lax.dot_general(left_terms(panel[:, :LANES], 0), right_terms(panel), (((0,), (0,)), ((), ())),
                                     preferred_element_type=jnp.float32)
            for u in range(at + 1 + AHEAD, slabs):
                tile[u] = tile[u] - update[SUB * u:SUB * u + SUB]
    factored = jnp.concatenate(done, axis=0)
    return jnp.where(col >= row, factored[:, :LANES], 0.0), factored[:, LANES:] if inverted else None


def factor_kernel(*refs, groups):
    strip_refs, (out_ref, gram_ref, factor_ref, column_ref, lead_ref, below_ref) = refs[:-6], refs[-6:]
    tiles = gram_ref.shape[0] // LANES
    height = LANES // STRIPS
    for group, pairs in enumerate(groups):
        for low_bit in range(2):
            for slot, strip in enumerate(strip_starts(group, low_bit)):
                for block, (upper, right) in enumerate(pairs):
                    gram_ref[pl.ds(upper * LANES + strip, height), right * LANES:(right + 1) * LANES] = strip_refs[
                        2 * group + low_bit][slot, block * height:(block + 1) * height, :]
    factor_ref[...] = jnp.zeros_like(factor_ref)
    for at in range(tiles):
        here = slice(at * LANES, (at + 1) * LANES)
        factor, inverse = factor_tile(gram_ref[here, here], column_ref, lead_ref, below_ref, at < tiles - 1)
        factor_ref[here, here] = factor
        if at < tiles - 1:
            rest = (at + 1) * LANES
            panel = times(inverse, gram_ref[here, rest:])
            factor_ref[here, rest:] = panel
            gram_ref[rest:, rest:] -= inner_product(panel, panel)
    width = out_ref.shape[1]
    first = pl.multiple_of(lax.axis_index("cols") * width, width)
    out_ref[...] = factor_ref[:, pl.ds(first, width)]


def factor_panel(strips, total, width):
    return pl.pallas_call(
        functools.partial(factor_kernel, groups=block_groups(total // LANES)),
        out_shape=jax.ShapeDtypeStruct((total, width), jnp.float32),
        scratch_shapes=[pltpu.VMEM((total, total), jnp.float32)] * 2 + [
            pltpu.VMEM((LANES * SUB, LANES), jnp.float32), pltpu.VMEM((2 * LANES, LANES), jnp.float32),
            pltpu.VMEM((LANES * SUB, LANES), jnp.float32)],
        compiler_params=pltpu.CompilerParams(vmem_limit_bytes=16 << 20),
    )(*strips)


def summed_strips(keep, send, group, bits):
    core, *order = strip_bits(group)
    gram = keep + swapped(send, "rows", core)
    for bit in order:
        half = gram.shape[0] // 2
        gram = gram[:half] + swapped(gram[half:], "rows", bit)
    for bit in range(len(order) + 1, bits):
        gram = gram + swapped(gram, "rows", bit)
    for bit in reversed(order):
        gram = jnp.concatenate([gram, swapped(gram, "rows", bit)])
    return [gram, swapped(gram, "rows", core)]


def reduce_run(keep, send, order):
    value = keep + swapped(send, "rows", 0)
    for bit in order:
        half = value.shape[0] // 2
        value = value[:half] + swapped(value[half:], "rows", bit)
    return value


def body(slab, sign_bits, block_mask, sample_rows):
    row_count, panel_width = slab.shape
    groups = lax.axis_size("rows")
    peers = lax.axis_size("cols")
    bits = groups.bit_length() - 1
    pick_count = sample_rows.shape[0]
    blocks = block_mask.shape[0]
    signs = (2 * sign_bits - 1).reshape(blocks, row_count // blocks) * block_mask.reshape(blocks, 1)
    signs = signs.reshape(row_count // LANES, LANES).astype(jnp.float32)
    picks = sample_rows
    for bit in range(bits):
        run = bit - (bits - 3)
        if run == 0:
            picks, signs = lax.optimization_barrier((picks, signs))
        other = swapped(picks, "rows", bit)
        if run == 0:
            low, rest = mix_first(slab, signs)
            other, low, rest = lax.optimization_barrier((other, low, rest))
        elif run == 1:
            high = mix_next(rest, signs)
            other, low, high = lax.optimization_barrier((other, low, high))
        elif run == 2:
            mixed = mix_join(low, high)
            other, mixed = lax.optimization_barrier((other, mixed))
        picks = jnp.concatenate([picks, other])
    first = pick_count // 2
    cross = list(range(1, bits))
    sketch = []
    pieces = []
    job_a = (0, first, cross)
    job_b = (first, pick_count - first, cross[1:2] + cross[:1] + cross[2:])
    send_a, = pick_rows(picks, mixed, [job_a + (1,)], groups)
    send_a, mixed = lax.optimization_barrier((send_a, mixed))
    keep_a, send_b, keep_b = pick_rows(picks, mixed, [job_a + (0,), job_b + (1,), job_b + (0,)], groups)
    for keep, send, order in ((keep_a, send_a, job_a[2]), (keep_b, send_b, job_b[2])):
        part = reduce_run(keep, send, order)
        sketch.append(part)
        pieces.append(part)
        for peer in range(1, peers):
            pieces.append(lax.ppermute(part, "cols", [(i, i ^ peer) for i in range(peers)]))
    sketch = jnp.concatenate(sketch)
    parts = partial_gram(pieces, pick_count, peers, 1.0 / (pick_count * groups))
    strips = []
    for group in range(len(parts) // 2):
        strips += summed_strips(parts[2 * group], parts[2 * group + 1], group, bits)
    r_panel = factor_panel(strips, panel_width * peers, panel_width)
    return (sketch, r_panel)


def solution(mesh):
    in_specs = (P("rows", "cols"), P("rows"), P("rows"), P("rows"))
    out_specs = (P("rows", "cols"), P(None, "cols"))
    return jax.shard_map(body, mesh=mesh, in_specs=in_specs, out_specs=out_specs, check_vma=False)
```
